32 devices in a mesh: sec: 2 (over core), row: 4 (over y, x), col: 4 (over z).
Axes of the slice: x: 2, y: 2, z: 4, core: 2. Of those that a mesh axis runs over, the one named last changes fastest.
Arguments:
- anc_inverse: float32 [2048, 2048], P('row', ('sec', 'col')), as said below
- panel: float32 [8192, 2048], P(('sec', 'col'), 'row'), may hold values from -0.5 to 0.5
- diag_inverse: float32 [8192, 512], P(('sec', 'col')), may hold values from -6 to 6
- widths: int32 [16], replicated, may hold values from 1 to 4, as said below
- pattern: int32 [16, 16], replicated, may hold values 0 or 1
Outputs:
- off_inverse: float32 [8192, 2048], P(('sec', 'col'), 'row')
- child_inverse: float32 [8192, 512], P(('sec', 'col'))
The draws below stay inside these ranges and needn't reach their ends.
Inputs may be any that keep to these rules, and one draw needn't show every extreme that they name: `anc_inverse`: exactly symmetric. `widths`: both 1 and 4 occur in every draw.
All inputs are finite; a program needn't handle non-finite values.
Results may differ from the reference program's by a relative error of at most 0.0003.
Values sent between devices are 32-bit elements; how exact they have to be, the bound alone decides.
A program may use at most 128 MiB of HBM per device.

```python
import math
import jax
import jax.numpy as jnp
from jax import lax

B = 128
WMAX = 4
SW = 512
NA = 2048
NAB = 16
SLOTS = 16
CHILD_COLS = 8192


def draw_anc_inverse(key, part):
    first_key, second_key = jax.random.split(jax.random.fold_in(key, 11), 2)
    rough = jax.random.normal(first_key, (NA, NA), jnp.float32)
    symmetric = (rough + rough.T) * (0.5 ** 0.5 / math.sqrt(NA))
    diagonal = jnp.exp(jax.random.uniform(second_key, (NA,), jnp.float32, 0.0, math.log(4.0)))
    return symmetric + jnp.diag(diagonal)


def draw_widths(key, part):
    first_key, second_key = jax.random.split(jax.random.fold_in(key, 23))
    drawn = jax.random.randint(first_key, (SLOTS,), 1, WMAX + 1)
    spots = jax.random.permutation(second_key, SLOTS)
    drawn = drawn.at[spots[0]].set(WMAX).at[spots[1]].set(1)
    return drawn.astype(jnp.int32)


def touch_ends(entries, own_key, smallest, largest):
    place = [jax.random.randint(jax.random.fold_in(own_key, axis), (), 0, length) for axis, length in enumerate(entries.shape)]
    longest = entries.shape.index(max(entries.shape))
    neighbour = place[:longest] + [(place[longest] + 1) % entries.shape[longest]] + place[longest + 1:]
    return entries.at[tuple(place)].set(smallest).at[tuple(neighbour)].set(largest)


def levels(key, extent, cuts, low, largest):
    level = 1.0
    for axis_at, blocks in cuts:
        draws = jax.random.uniform(jax.random.fold_in(jax.random.fold_in(key, 6), axis_at), (blocks,), jnp.float32, low / len(cuts), largest / len(cuts))
        level = level * jnp.repeat(jnp.exp(draws), extent[axis_at] // blocks).reshape((-1,) + (1,) * (len(extent) - 1 - axis_at))
    return level


def gaussian(rng, shape, deviation, most, shards=(), kind=jnp.bfloat16):
    result = jax.random.normal(rng, shape, jnp.float32) * deviation
    if len(shards) > 0:
        result = levels(rng, shape, shards, -0.22, 0.18) * result
    return jnp.clip(result, min=-most, max=most).astype(kind)


def setup_inputs(seed: int = 0) -> dict:
    key_list = jax.random.split(jax.random.key(seed), 6)
    return {
        "anc_inverse": draw_anc_inverse(jax.random.fold_in(key_list[5], 71), 0),
        "panel": gaussian(key_list[1], (CHILD_COLS, NA), (NA // 16) ** -0.5, 0.5, ((0, 8), (1, 4)), jnp.float32),
        "diag_inverse": gaussian(key_list[2], (CHILD_COLS, SW), 1.0, 6.0, ((0, 8),), jnp.float32),
        "widths": draw_widths(jax.random.fold_in(key_list[5], 71), 0),
        "pattern": touch_ends((jax.random.randint(key_list[4], (SLOTS, NAB), 0, 2) < 1).astype(jnp.int32), jax.random.fold_in(key_list[4], 1), 0, 1),
    }


def reference(anc_inverse, panel, diag_inverse, widths, pattern):
    highest = lax.Precision.HIGHEST
    position = jnp.arange(SW, dtype=jnp.int32)

    def solve_slot(inputs):
        slot_panel, slot_diag, slot_blocks, slot_pattern = inputs
        column_mask = (position < slot_blocks * B).astype(jnp.float32)
        row_mask = jnp.repeat(slot_pattern.astype(jnp.float32), B)
        masked = slot_panel * column_mask[:, None] * row_mask[None, :]
        product = jnp.dot(masked, anc_inverse, precision=highest, preferred_element_type=jnp.float32)
        product = product * column_mask[:, None] * row_mask[None, :]
        update = jnp.dot(product, masked.T, precision=highest, preferred_element_type=jnp.float32)
        diag_block = (slot_diag + update) * column_mask[:, None] * column_mask[None, :]
        return -product, diag_block

    off_blocks, diag_blocks = lax.map(
        solve_slot,
        (panel.reshape(SLOTS, SW, NA), diag_inverse.reshape(SLOTS, SW, SW), widths, pattern),
    )
    return off_blocks.reshape(SLOTS * SW, NA), diag_blocks.reshape(SLOTS * SW, SW)
```

```python
import functools
import jax
import jax.numpy as jnp
from jax import lax
from jax.experimental import pallas as pl
from jax.experimental.pallas import tpu as pltpu
from jax.sharding import PartitionSpec as P

B = 128
SW = 512
CHUNKS = 8
OCHUNKS = 4
TM = 256
F32 = jnp.float32
BF = jnp.bfloat16
MESH = pl.DeviceIdType.MESH
NN = (((1,), (0,)), ((), ()))
NT = (((1,), (1,)), ((), ()))


def split(value):
    high = value.astype(BF)
    return high, (value - high.astype(F32)).astype(BF)


def dot3(ah, al, bh, bl, dims):
    dot = functools.partial(lax.dot_general, dimension_numbers=dims, preferred_element_type=F32)
    return dot(ah, bh) + (dot(ah, bl) + dot(al, bh))


def packed_rows(nrow):
    wb = SW // B
    return (wb * (wb + 1) // 2 - wb // 2) * B + 8 * nrow


def factor(count):
    low = 1
    for value in range(1, count + 1):
        if count % value == 0 and value * value <= count:
            low = value
    return count // low, low


class Group:
    def __init__(self, copies):
        self.copies = copies

    def start(self):
        for one in self.copies:
            one.start()

    def wait_recv(self):
        for one in self.copies:
            one.wait_recv()

    def wait_send(self):
        for one in self.copies:
            one.wait_send()


def kernel(
    sizes,
    anc_ref, panel_ref, diag_ref, widths_ref, pattern_ref, prod_ref, upd_ref,
    anc, ah, al, ph, plo, pin, opp, oh, ol, qsend, qrecv, upack, urecv, usum, urecv2, ufin,
    zs, zr, ps, pr, os_, or_, qs, qr, us, ur, us2, ur2, gs2, gr2, gs, gr, ds, crossed,
):
    nsec, nrow, ncol, nf, ns, nb, square = sizes
    rows, width = panel_ref.shape
    pw = anc_ref.shape[1]
    per = width // pw
    slots = rows // SW
    wb = SW // B
    part = packed_rows(nrow) // nrow
    tm = TM
    parts = SW // tm
    sec, row, col = lax.axis_index("sec"), lax.axis_index("row"), lax.axis_index("col")
    turn = sec if square else 0
    a, b = row // nb, row % nb
    f = a + turn * (b - a)
    s = b + turn * (a - b)
    cf = nb - turn * (nb - 1)
    cs = 1 + turn * (nb - 1)

    def at(fi, si):
        return fi * cf + si * cs

    def copy(src, dst, send, recv, where):
        return pltpu.make_async_remote_copy(
            src_ref=src, dst_ref=dst, send_sem=send, recv_sem=recv, device_id=where, device_id_type=MESH
        )

    first = (sec * ncol + col) * slots
    blocks = width // B
    fill = [widths_ref[first + j] for j in range(slots)]
    load_diag = pltpu.make_async_copy(diag_ref, upd_ref, ds)

    def inside(j, i):
        return jnp.where(fill[j] > i, 1.0, 0.0).astype(F32)

    def present(j, r, c):
        return pattern_ref[first + j, r * blocks + c].astype(F32)

    def keep(src, j, h, slot, r):
        for i in range(h * wb // parts, (h + 1) * wb // parts):
            here = pl.ds(j * SW + i * B, B)
            for c in range(blocks):
                cols = pl.ds(c * B, B)
                high, low = split(src(i, cols) * (inside(j, i) * present(j, r, c)))
                ph[slot, here, cols] = high
                plo[slot, here, cols] = low

    has_left = (col > 0).astype(jnp.int32)
    has_right = (col < ncol - 1).astype(jnp.int32)
    barrier = pltpu.get_barrier_semaphore()
    for d in range(1, nrow):
        pl.semaphore_signal(barrier, inc=1, device_id={"row": (row + d) % nrow}, device_id_type=MESH)
    pl.semaphore_signal(barrier, inc=1, device_id={"sec": 1 - sec}, device_id_type=MESH)

    @pl.when(col > 0)
    def _():
        pl.semaphore_signal(barrier, inc=1, device_id={"col": col - 1}, device_id_type=MESH)

    @pl.when(col < ncol - 1)
    def _():
        pl.semaphore_signal(barrier, inc=1, device_id={"col": col + 1}, device_id_type=MESH)

    pl.semaphore_wait(barrier, nrow + has_left + has_right)

    mine = sec * ncol + col

    def piece_copy(src, p, way):
        where = ({"col": col - 1}, {"col": col + 1}, {"sec": 1 - sec})[way]
        size = src.shape[0] // CHUNKS
        return Group([
            copy(
                src.at[pl.ds(c * size, size)], anc.at[p, pl.ds(c * size, size)],
                zs.at[p, way, c], zr.at[p, c], where,
            )
            for c in range(CHUNKS)
        ])

    def opp_copy(src, d, e, k):
        return copy(
            src, opp.at[d - 1, e - 1, k], os_.at[d - 1, e - 1, k], or_.at[d - 1, e - 1, k],
            {"row": at((f + d) % nf, s)},
        )

    def pass_on(src, p):
        for d in range(1, nf):
            for e in range(1, ns):
                @pl.when(p // per == at((f + d) % nf, (s + e) % ns))
                def _():
                    opp_copy(src, d, e, p % per).start()

    def panel_copy(d, j, h):
        return copy(
            panel_ref.at[pl.ds(j * SW + h * tm, tm)], pin.at[d - 1, j, pl.ds(h * tm, tm)],
            ps.at[d - 1, j, h], pr.at[d - 1, j, h], {"row": at((f + d) % nf, s)},
        )

    def halves(src, p):
        high, low = split(src[...])
        ah[p] = high
        al[p] = low

    def late(p):
        return p // per == row

    def send_mine():
        pl.when(col > 0)(lambda: piece_copy(anc_ref, mine, 0).start())
        pl.when(col < ncol - 1)(lambda: piece_copy(anc_ref, mine, 1).start())
        piece_copy(anc_ref, mine, 2).start()

    other = (1 - sec) * ncol + col

    def panels_out():
        for j in range(slots):
            for h in range(parts):
                for d in range(1, nf):
                    panel_copy(d, j, h).start()

    def settle_own():
        load_diag.start()
        halves(anc_ref, mine)
        for j in range(slots):
            for h in range(parts):
                keep(lambda i, cols: panel_ref[pl.ds(j * SW + i * B, B), cols], j, h, 0, row)

    def relay(p, way, c, onward):
        piece_copy(anc_ref, p, way).copies[c].wait_recv()
        pl.when(onward)(lambda: piece_copy(anc.at[p], p, way).copies[c].start())
        piece_copy(anc.at[p], p, 2).copies[c].start()

    if crossed is not None:
        obuf, xs, xr, zos, zor = crossed
        half = width // 2
        osize = half // OCHUNKS

        def native(z):
            return (z // per != b).astype(jnp.int32)

        def early(side, z):
            return native(z) == (side == a).astype(jnp.int32)

        def cross_copies(axis):
            where = {"row": (1 - a) * nb + b} if axis == 0 else {"row": a * nb + 1 - b}
            k = col % per
            base = (k if axis == 0 else 1 - k) * half
            return Group([
                copy(
                    anc_ref.at[pl.ds(pl.multiple_of(base + c * osize, 8), osize)],
                    obuf.at[col, pl.ds(c * osize, osize)], xs.at[axis, c], xr.at[c], where,
                )
                for c in range(OCHUNKS)
            ])

        def o_copy(z, way):
            where = ({"col": col - 1}, {"col": col + 1}, {"sec": 1 - sec})[way]
            return Group([
                copy(
                    obuf.at[z, pl.ds(c * osize, osize)], obuf.at[z, pl.ds(c * osize, osize)],
                    zos.at[z, way, c], zor.at[z, c], where,
                )
                for c in range(OCHUNKS)
            ])

        is_early = early(sec, col)
        is_opp = jnp.logical_and(native(col) == 1, sec != a)

        @pl.when(is_opp)
        def _():
            cross_copies(0).start()
            cross_copies(1).start()

        pl.when(is_early)(send_mine)
        panels_out()
        settle_own()

        @pl.when(is_early)
        def _():
            for c in range(OCHUNKS):
                cross_copies(0).copies[c].wait_recv()
                pl.when(col > 0)(lambda: o_copy(col, 0).copies[c].start())
                pl.when(col < ncol - 1)(lambda: o_copy(col, 1).copies[c].start())
                o_copy(col, 2).copies[c].start()

        def o_relay(z, way, c, onward):
            o_copy(z, way).copies[c].wait_recv()
            pl.when(onward)(lambda: o_copy(z, way).copies[c].start())
            o_copy(z, 2).copies[c].start()

        def from_partner(z):
            p = (1 - sec) * ncol + z
            piece_copy(anc_ref, p, 2).wait_recv()
            o_copy(z, 2).wait_recv()
            halves(anc.at[p], p)

        def early_step(t, carry):
            left = jnp.logical_and(col - t >= 0, early(sec, col - t))
            right = jnp.logical_and(col + t < ncol, early(sec, col + t))
            for c in range(CHUNKS):
                pl.when(left)(lambda: relay(mine - t, 1, c, col < ncol - 1))
                pl.when(right)(lambda: relay(mine + t, 0, c, col > 0))
            for c in range(OCHUNKS):
                pl.when(left)(lambda: o_relay(col - t, 1, c, col < ncol - 1))
                pl.when(right)(lambda: o_relay(col + t, 0, c, col > 0))
            pl.when(left)(lambda: halves(anc.at[mine - t], mine - t))
            pl.when(right)(lambda: halves(anc.at[mine + t], mine + t))
            left = jnp.logical_and(col - t >= 0, early(1 - sec, col - t))
            right = jnp.logical_and(col + t < ncol, early(1 - sec, col + t))
            pl.when(left)(lambda: from_partner(col - t))
            pl.when(right)(lambda: from_partner(col + t))
            return carry

        pl.when(early(1 - sec, col))(lambda: from_partner(col))
        lax.fori_loop(1, ncol, early_step, 0)
        pl.when(late(mine))(send_mine)

        for z in range(ncol):
            k = z % per
            seen = native(z)
            turned = seen == sec
            rpos = jnp.where(jnp.logical_or(seen == 1, sec == 0), k, 1 - k)
            cpos = jnp.where(jnp.logical_or(seen == 1, sec == 1), k, 1 - k)
            here = pl.ds(pl.multiple_of(rpos * half, half), half)

            def place(value):
                high, low = split(value)
                oh[0, 0, cpos, here] = high
                ol[0, 0, cpos, here] = low

            pl.when(turned)(lambda: place(obuf[z].T))
            pl.when(jnp.logical_not(turned))(lambda: place(obuf[z]))

        def late_partner(p):
            piece_copy(anc_ref, p, 2).wait_recv()
            halves(anc.at[p], p)

        def late_step(t):
            left = jnp.logical_and(col - t >= 0, late(mine - t))
            right = jnp.logical_and(col + t < ncol, late(mine + t))
            for c in range(CHUNKS):
                pl.when(left)(lambda: relay(mine - t, 1, c, col < ncol - 1))
                pl.when(right)(lambda: relay(mine + t, 0, c, col > 0))
            pl.when(left)(lambda: halves(anc.at[mine - t], mine - t))
            pl.when(right)(lambda: halves(anc.at[mine + t], mine + t))
            left = jnp.logical_and(col - t >= 0, late(other - t))
            right = jnp.logical_and(col + t < ncol, late(other + t))
            pl.when(left)(lambda: late_partner(other - t))
            pl.when(right)(lambda: late_partner(other + t))

        def late_work(spot):
            if spot == 0:
                pl.when(late(other))(lambda: late_partner(other))
            elif spot < slots * parts:
                if spot < ncol:
                    late_step(spot)

        def late_rest():
            for t in range(slots * parts, ncol):
                late_step(t)
    else:
        @pl.when(jnp.logical_not(late(mine)))
        def _():
            send_mine()
            pass_on(anc_ref, mine)

        panels_out()
        settle_own()

        def settle(p):
            pass_on(anc.at[p], p)
            halves(anc.at[p], p)

        def from_partner(p):
            piece_copy(anc_ref, p, 2).wait_recv()
            pass_on(anc.at[p], p)
            halves(anc.at[p], p)

        def gather(phase):
            def ready(p):
                return late(p) if phase else jnp.logical_not(late(p))

            def step(t, carry):
                left = jnp.logical_and(col - t >= 0, ready(mine - t))
                right = jnp.logical_and(col + t < ncol, ready(mine + t))
                for c in range(CHUNKS):
                    pl.when(left)(lambda: relay(mine - t, 1, c, col < ncol - 1))
                    pl.when(right)(lambda: relay(mine + t, 0, c, col > 0))
                pl.when(left)(lambda: settle(mine - t))
                pl.when(right)(lambda: settle(mine + t))
                partners(t)
                return carry

            def partners(t):
                left = jnp.logical_and(col - t >= 0, ready(other - t))
                right = jnp.logical_and(col + t < ncol, ready(other + t))
                pl.when(left)(lambda: from_partner(other - t))
                pl.when(jnp.logical_and(right, t > 0))(lambda: from_partner(other + t))

            partners(0)
            lax.fori_loop(1, ncol, step, 0)

        gather(0)
        pl.when(late(mine))(send_mine)
        for d in range(1, nf):
            for e in range(1, ns):
                for k in range(per):
                    opp_copy(anc_ref, d, e, k).wait_recv()
                    high, low = split(opp[d - 1, e - 1, k])
                    oh[d - 1, e - 1, k] = high
                    ol[d - 1, e - 1, k] = low

        def late_work(spot):
            pass

        def late_rest():
            gather(1)

    def q_copy(e, j, h):
        rr = pl.ds(h * tm, tm)
        return copy(
            qsend.at[e - 1, j, rr], qrecv.at[e - 1, j, rr], qs.at[e - 1, j, h], qr.at[e - 1, j, h],
            {"row": at(f, (s + e) % ns)},
        )

    for j in range(slots):
        for h in range(parts):
            for d in range(1, nf):
                panel_copy(d, j, h).wait_recv()
                keep(lambda i, cols: pin[d - 1, j, pl.ds(i * B, B), cols], j, h, d, at((f + nf - d) % nf, s))
            rr = pl.ds(j * SW + h * tm, tm)
            for e in range(1, ns):
                base = at(f, (s + e) % ns) * per
                for k in range(per):
                    acc = dot3(ph[0, rr], plo[0, rr], ah[base + k], al[base + k], NN)
                    for d in range(1, nf):
                        acc += dot3(ph[d, rr], plo[d, rr], oh[d - 1, e - 1, k], ol[d - 1, e - 1, k], NN)
                    qsend[e - 1, j, pl.ds(h * tm, tm), pl.ds(k * pw, pw)] = acc
                q_copy(e, j, h).start()
            late_work(j * parts + h)

    def near(i, carry):
        rr = pl.ds(pl.multiple_of(i * tm, tm), tm)
        acc = jnp.zeros((tm, width), F32)
        for d in range(1, nf):
            for k in range(per):
                p = at((f + nf - d) % nf, s) * per + k
                cols = pl.ds(k * pw, pw)
                acc += dot3(ph[d, rr, cols], plo[d, rr, cols], ah[p], al[p], NT)
        prod_ref[rr] = acc
        return carry

    lax.fori_loop(0, rows // tm, near, 0)
    late_rest()

    def own(i, carry):
        rr = pl.ds(pl.multiple_of(i * tm, tm), tm)
        for k in range(per):
            p = row * per + k
            prod_ref[rr, pl.ds(k * pw, pw)] += dot3(ph[0, rr], plo[0, rr], ah[p], al[p], NN)
        return carry

    lax.fori_loop(0, rows // tm, own, 0)

    span = nf * part

    def portion(i):
        return pl.ds(pl.multiple_of(i * span, 8), span)

    def across(d):
        return {"row": at(f, (s + d) % ns)}

    def along(d):
        return {"row": at((f + d) % nf, s)}

    def u_copy(j, d):
        return copy(
            upack.at[j, portion((s + d) % ns)], urecv.at[j, d - 1], us.at[j, d - 1], ur.at[j, d - 1], across(d)
        )

    def v_copy(j, d):
        return copy(
            usum.at[j, pl.ds(pl.multiple_of(((f + d) % nf) * part, 8), part)],
            urecv2.at[j, d - 1], us2.at[j, d - 1], ur2.at[j, d - 1], along(d),
        )

    def h_copy(j, d):
        done = pl.ds(pl.multiple_of((s * nf + f) * part, 8), part)
        return copy(ufin.at[j, done], ufin.at[j, done], gs2.at[j, d - 1], gr2.at[j, d - 1], along(d))

    def g_copy(j, d):
        return copy(ufin.at[j, portion(s)], ufin.at[j, portion(s)], gs.at[j, d - 1], gr.at[j, d - 1], across(d))

    ri = lax.broadcasted_iota(jnp.int32, (B, B), 0)
    ci = lax.broadcasted_iota(jnp.int32, (B, B), 1)
    rows8 = lax.broadcasted_iota(jnp.int32, (8, B), 0)
    pairs = wb // 2
    offs = {}
    for i in range(wb):
        for k in range(i + 1, wb):
            offs[i, k] = (pairs + len(offs)) * B
    tail = (pairs + len(offs)) * B

    def update_out(j):
        for h in range(parts):
            rr = pl.ds(j * SW + h * tm, tm)
            for e in range(1, ns):
                q_copy(e, j, h).wait_recv()
                prod_ref[rr] += qrecv[e - 1, j, pl.ds(h * tm, tm)]
        extra = jnp.zeros((8, B), F32)
        held = None
        for i in range(wb):
            qh, ql = split(prod_ref[pl.ds(j * SW + i * B, B)])
            rest = pl.ds(j * SW + i * B, SW - i * B)
            line = dot3(qh, ql, ph[0, rest], plo[0, rest], NT)
            for k in range(i + 1, wb):
                upack[j, pl.ds(offs[i, k], B)] = line[:, (k - i) * B:(k - i + 1) * B]
            if i % 2 == 0:
                held = line[:, :B]
            else:
                low = line[:, :B]
                upack[j, pl.ds(i // 2 * B, B)] = jnp.where(ri <= ci, held, low)
                mid = jnp.sum(jnp.where(ri == ci, low, 0.0), axis=0, keepdims=True)
                extra = jnp.where(rows8 == i // 2, mid, extra)
        upack[j, pl.ds(tail, 8)] = extra
        upack[j, pl.ds(tail + 8, 8 * (nrow - 1))] = jnp.zeros((8 * (nrow - 1), B), F32)
        for d in range(1, ns):
            u_copy(j, d).start()

    def second(j):
        for d in range(1, ns):
            u_copy(j, d).wait_recv()
        total = upack[j, portion(s)]
        for d in range(1, ns):
            total += urecv[j, d - 1]
        usum[j] = total
        for d in range(1, nf):
            v_copy(j, d).start()

    def third(j):
        for d in range(1, nf):
            v_copy(j, d).wait_recv()
        total = usum[j, pl.ds(pl.multiple_of(f * part, 8), part)]
        for d in range(1, nf):
            total += urecv2[j, d - 1]
        ufin[j, pl.ds(pl.multiple_of((s * nf + f) * part, 8), part)] = total
        for d in range(1, nf):
            h_copy(j, d).start()

    def fourth(j):
        for d in range(1, nf):
            h_copy(j, d).wait_recv()
        for d in range(1, ns):
            g_copy(j, d).start()

    def negate(j):
        for i in range(wb):
            here = pl.ds(j * SW + i * B, B)
            for c in range(blocks):
                cols = pl.ds(c * B, B)
                prod_ref[here, cols] = prod_ref[here, cols] * -(inside(j, i) * present(j, row, c))

    def finish(j):
        for d in range(1, ns):
            g_copy(j, d).wait_recv()
        for i in range(wb):
            both = ufin[j, pl.ds(i // 2 * B, B)]
            if i % 2 == 0:
                block = jnp.where(ri <= ci, both, both.T)
            else:
                block = jnp.where(ri > ci, both, both.T)
                block = jnp.where(ri == ci, ufin[j, pl.ds(tail + i // 2, 1)], block)
            here = (pl.ds(j * SW + i * B, B), pl.ds(i * B, B))
            upd_ref[here] = (upd_ref[here] + block) * inside(j, i)
            for k in range(i + 1, wb):
                block = ufin[j, pl.ds(offs[i, k], B)]
                upper = (pl.ds(j * SW + i * B, B), pl.ds(k * B, B))
                upd_ref[upper] = (upd_ref[upper] + block) * inside(j, k)
                lower = (pl.ds(j * SW + k * B, B), pl.ds(i * B, B))
                upd_ref[lower] = (upd_ref[lower] + block.T) * inside(j, k)

    stages = [update_out, second, third, fourth]
    for step in range(2 * (slots - 1) + len(stages)):
        for j in range(slots):
            if 0 <= step - 2 * j < len(stages):
                stages[step - 2 * j](j)
    for j in range(slots):
        negate(j)
    load_diag.wait()
    for j in range(slots):
        finish(j)

    for j in range(slots):
        for d in range(1, ns):
            u_copy(j, d).wait_send()
            g_copy(j, d).wait_send()
        for d in range(1, nf):
            v_copy(j, d).wait_send()
            h_copy(j, d).wait_send()
        for h in range(parts):
            for e in range(1, ns):
                q_copy(e, j, h).wait_send()
            for d in range(1, nf):
                panel_copy(d, j, h).wait_send()

    if crossed is None:
        for d in range(1, nf):
            for e in range(1, ns):
                for k in range(per):
                    opp_copy(anc_ref, d, e, k).wait_send()

    def drain(q, carry):
        p = sec * ncol + q
        to_right = jnp.logical_and(q <= col, col < ncol - 1)
        to_left = jnp.logical_and(q >= col, col > 0)
        if crossed is None:
            sent = q >= 0
        else:
            sent = jnp.logical_or(early(sec, q), late(p))
        pl.when(jnp.logical_and(sent, to_right))(lambda: piece_copy(anc_ref, p, 1).wait_send())
        pl.when(jnp.logical_and(sent, to_left))(lambda: piece_copy(anc_ref, p, 0).wait_send())
        pl.when(sent)(lambda: piece_copy(anc_ref, p, 2).wait_send())
        if crossed is not None:
            first_half = early(sec, q)
            pl.when(jnp.logical_and(first_half, to_right))(lambda: o_copy(q, 1).wait_send())
            pl.when(jnp.logical_and(first_half, to_left))(lambda: o_copy(q, 0).wait_send())
            pl.when(first_half)(lambda: o_copy(q, 2).wait_send())
        return carry

    lax.fori_loop(0, ncol, drain, 0)
    if crossed is not None:
        @pl.when(is_opp)
        def _():
            cross_copies(0).wait_send()
            cross_copies(1).wait_send()


def local(sizes, anc_inverse, panel, diag_inverse, widths, pattern):
    nsec, nrow, ncol, nf, ns, nb, square = sizes
    rows, width = panel.shape
    pw = anc_inverse.shape[1]
    per = width // pw
    slots = rows // SW
    pieces = nsec * ncol
    packed = packed_rows(nrow)
    part = packed // nrow
    parts = SW // TM
    short = square and nsec == nb == per == 2 and ncol == per * nb
    vm = pltpu.VMEM
    dma = pltpu.SemaphoreType.DMA
    whole = pl.BlockSpec(memory_space=pltpu.VMEM)
    scalar = pl.BlockSpec(memory_space=pltpu.SMEM)
    return pl.pallas_call(
        functools.partial(kernel, sizes),
        out_shape=(jax.ShapeDtypeStruct((rows, width), F32), jax.ShapeDtypeStruct((rows, SW), F32)),
        in_specs=[whole, whole, pl.BlockSpec(memory_space=pl.ANY), scalar, scalar],
        out_specs=(whole, whole),
        scratch_shapes=[
            vm((pieces, width, pw), F32),
            vm((pieces, width, pw), BF),
            vm((pieces, width, pw), BF),
            vm((nf, rows, width), BF),
            vm((nf, rows, width), BF),
            vm((nf - 1, slots, SW, width), F32),
            None if short else vm((nf - 1, ns - 1, per, width, pw), F32),
            vm((nf - 1, ns - 1, per, width, pw), BF),
            vm((nf - 1, ns - 1, per, width, pw), BF),
            vm((ns - 1, slots, SW, width), F32),
            vm((ns - 1, slots, SW, width), F32),
            vm((slots, packed, B), F32),
            vm((slots, ns - 1, nf * part, B), F32),
            vm((slots, nf * part, B), F32),
            vm((slots, nf - 1, part, B), F32),
            vm((slots, packed, B), F32),
            dma((pieces, 3, CHUNKS)), dma((pieces, CHUNKS)),
            dma((nf - 1, slots, parts)), dma((nf - 1, slots, parts)),
            None if short else dma((nf - 1, ns - 1, per)), None if short else dma((nf - 1, ns - 1, per)),
            dma((ns - 1, slots, parts)), dma((ns - 1, slots, parts)),
            dma((slots, ns - 1)), dma((slots, ns - 1)),
            dma((slots, nf - 1)), dma((slots, nf - 1)),
            dma((slots, nf - 1)), dma((slots, nf - 1)),
            dma((slots, ns - 1)), dma((slots, ns - 1)),
            dma,
            (
                vm((ncol, width // 2, pw), F32), dma((2, OCHUNKS)), dma((OCHUNKS,)),
                dma((ncol, 3, OCHUNKS)), dma((ncol, OCHUNKS)),
            ) if short else None,
        ],
        compiler_params=pltpu.CompilerParams(
            collective_id=0, has_side_effects=True, vmem_limit_bytes=60 * 1024 * 1024
        ),
    )(anc_inverse, panel, diag_inverse, widths, pattern)


def solution(mesh):
    shape = dict(mesh.shape)
    na, nb = factor(shape["row"])
    sizes = (shape["sec"], shape["row"], shape["col"], na, nb, nb, na == nb)
    in_specs = (
        P("row", ("sec", "col")),
        P(("sec", "col"), "row"),
        P(("sec", "col"), None),
        P(),
        P(),
    )
    out_specs = (P(("sec", "col"), "row"), P(("sec", "col"), None))
    return jax.shard_map(
        functools.partial(local, sizes), mesh=mesh, in_specs=in_specs, out_specs=out_specs, check_vma=False
    )
```

```python
import functools
import jax
import jax.numpy as jnp
from jax import lax
from jax.experimental import pallas as pl
from jax.experimental.pallas import tpu as pltpu
from jax.sharding import PartitionSpec as P

B = 128
SW = 512
CHUNKS = 8
OCHUNKS = 4
TM = 256
F32 = jnp.float32
BF = jnp.bfloat16
MESH = pl.DeviceIdType.MESH
NN = (((1,), (0,)), ((), ()))
NT = (((1,), (1,)), ((), ()))


def split(value):
    high = value.astype(BF)
    return high, (value - high.astype(F32)).astype(BF)


def dot3(ah, al, bh, bl, dims):
    dot = functools.partial(lax.dot_general, dimension_numbers=dims, preferred_element_type=F32)
    return dot(ah, bh) + (dot(ah, bl) + dot(al, bh))


def packed_rows(nrow):
    wb = SW // B
    return (wb * (wb + 1) // 2 - wb // 2) * B + 8 * nrow


def spots(wb):
    offs = {}
    for i in range(wb):
        for k in range(i + 1, wb):
            offs[i, k] = (wb // 2 + len(offs)) * B
    return offs, (wb // 2 + len(offs)) * B


def factor(count):
    low = 1
    for value in range(1, count + 1):
        if count % value == 0 and value * value <= count:
            low = value
    return count // low, low


class Group:
    def __init__(self, copies):
        self.copies = copies

    def start(self):
        for one in self.copies:
            one.start()

    def wait_recv(self):
        for one in self.copies:
            one.wait_recv()

    def wait_send(self):
        for one in self.copies:
            one.wait_send()


def kernel(
    sizes,
    anc_ref, panel_ref, widths_ref, pattern_ref, prod_ref, sum_ref,
    anc, ah, al, ph, plo, pin, opp, oh, ol, qsend, qrecv, upack, urecv, usum, urecv2, ufin,
    zs, zr, ps, pr, os_, or_, qs, qr, us, ur, us2, ur2, gs2, gr2, gs, gr, crossed,
):
    nsec, nrow, ncol, nf, ns, nb, square = sizes
    rows, width = panel_ref.shape
    pw = anc_ref.shape[1]
    per = width // pw
    slots = rows // SW
    wb = SW // B
    part = packed_rows(nrow) // nrow
    tm = TM
    parts = SW // tm
    sec, row, col = lax.axis_index("sec"), lax.axis_index("row"), lax.axis_index("col")
    turn = sec if square else 0
    a, b = row // nb, row % nb
    f = a + turn * (b - a)
    s = b + turn * (a - b)
    cf = nb - turn * (nb - 1)
    cs = 1 + turn * (nb - 1)

    def at(fi, si):
        return fi * cf + si * cs

    def copy(src, dst, send, recv, where):
        return pltpu.make_async_remote_copy(
            src_ref=src, dst_ref=dst, send_sem=send, recv_sem=recv, device_id=where, device_id_type=MESH
        )

    first = (sec * ncol + col) * slots
    blocks = width // B
    fill = [widths_ref[first + j] for j in range(slots)]

    def inside(j, i):
        return jnp.where(fill[j] > i, 1.0, 0.0).astype(F32)

    def present(j, r, c):
        return pattern_ref[first + j, r * blocks + c].astype(F32)

    def keep(src, j, h, slot, r):
        for i in range(h * wb // parts, (h + 1) * wb // parts):
            here = pl.ds(j * SW + i * B, B)
            for c in range(blocks):
                cols = pl.ds(c * B, B)
                high, low = split(src(i, cols) * (inside(j, i) * present(j, r, c)))
                ph[slot, here, cols] = high
                plo[slot, here, cols] = low

    has_left = (col > 0).astype(jnp.int32)
    has_right = (col < ncol - 1).astype(jnp.int32)
    barrier = pltpu.get_barrier_semaphore()
    for d in range(1, nrow):
        pl.semaphore_signal(barrier, inc=1, device_id={"row": (row + d) % nrow}, device_id_type=MESH)
    pl.semaphore_signal(barrier, inc=1, device_id={"sec": 1 - sec}, device_id_type=MESH)

    @pl.when(col > 0)
    def _():
        pl.semaphore_signal(barrier, inc=1, device_id={"col": col - 1}, device_id_type=MESH)

    @pl.when(col < ncol - 1)
    def _():
        pl.semaphore_signal(barrier, inc=1, device_id={"col": col + 1}, device_id_type=MESH)

    pl.semaphore_wait(barrier, nrow + has_left + has_right)

    mine = sec * ncol + col

    def piece_copy(src, p, way):
        where = ({"col": col - 1}, {"col": col + 1}, {"sec": 1 - sec})[way]
        size = src.shape[0] // CHUNKS
        return Group([
            copy(
                src.at[pl.ds(c * size, size)], anc.at[p, pl.ds(c * size, size)],
                zs.at[p, way, c], zr.at[p, c], where,
            )
            for c in range(CHUNKS)
        ])

    def opp_copy(src, d, e, k):
        return copy(
            src, opp.at[d - 1, e - 1, k], os_.at[d - 1, e - 1, k], or_.at[d - 1, e - 1, k],
            {"row": at((f + d) % nf, s)},
        )

    def pass_on(src, p):
        for d in range(1, nf):
            for e in range(1, ns):
                @pl.when(p // per == at((f + d) % nf, (s + e) % ns))
                def _():
                    opp_copy(src, d, e, p % per).start()

    def panel_copy(d, j, h):
        return copy(
            panel_ref.at[pl.ds(j * SW + h * tm, tm)], pin.at[d - 1, j, pl.ds(h * tm, tm)],
            ps.at[d - 1, j, h], pr.at[d - 1, j, h], {"row": at((f + d) % nf, s)},
        )

    def halves(src, p):
        high, low = split(src[...])
        ah[p] = high
        al[p] = low

    def late(p):
        return p // per == row

    def send_mine():
        pl.when(col > 0)(lambda: piece_copy(anc_ref, mine, 0).start())
        pl.when(col < ncol - 1)(lambda: piece_copy(anc_ref, mine, 1).start())
        piece_copy(anc_ref, mine, 2).start()

    other = (1 - sec) * ncol + col

    def panels_out():
        for j in range(slots):
            for h in range(parts):
                for d in range(1, nf):
                    panel_copy(d, j, h).start()

    def settle_own():
        halves(anc_ref, mine)
        for j in range(slots):
            for h in range(parts):
                keep(lambda i, cols: panel_ref[pl.ds(j * SW + i * B, B), cols], j, h, 0, row)

    def relay(p, way, c, onward):
        piece_copy(anc_ref, p, way).copies[c].wait_recv()
        pl.when(onward)(lambda: piece_copy(anc.at[p], p, way).copies[c].start())
        piece_copy(anc.at[p], p, 2).copies[c].start()

    if crossed is not None:
        obuf, xs, xr, zos, zor = crossed
        half = width // 2
        osize = half // OCHUNKS

        def native(z):
            return (z // per != b).astype(jnp.int32)

        def early(side, z):
            return native(z) == (side == a).astype(jnp.int32)

        def cross_copies(axis):
            where = {"row": (1 - a) * nb + b} if axis == 0 else {"row": a * nb + 1 - b}
            k = col % per
            base = (k if axis == 0 else 1 - k) * half
            return Group([
                copy(
                    anc_ref.at[pl.ds(pl.multiple_of(base + c * osize, 8), osize)],
                    obuf.at[col, pl.ds(c * osize, osize)], xs.at[axis, c], xr.at[c], where,
                )
                for c in range(OCHUNKS)
            ])

        def o_copy(z, way):
            where = ({"col": col - 1}, {"col": col + 1}, {"sec": 1 - sec})[way]
            return Group([
                copy(
                    obuf.at[z, pl.ds(c * osize, osize)], obuf.at[z, pl.ds(c * osize, osize)],
                    zos.at[z, way, c], zor.at[z, c], where,
                )
                for c in range(OCHUNKS)
            ])

        is_early = early(sec, col)
        is_opp = jnp.logical_and(native(col) == 1, sec != a)

        @pl.when(is_opp)
        def _():
            cross_copies(0).start()
            cross_copies(1).start()

        at_end = jnp.logical_or(col == 0, col == ncol - 1)
        pl.when(is_early)(send_mine)
        panels_out()
        pl.when(jnp.logical_and(late(mine), at_end))(send_mine)
        settle_own()

        @pl.when(is_early)
        def _():
            for c in range(OCHUNKS):
                cross_copies(0).copies[c].wait_recv()
                pl.when(col > 0)(lambda: o_copy(col, 0).copies[c].start())
                pl.when(col < ncol - 1)(lambda: o_copy(col, 1).copies[c].start())
                o_copy(col, 2).copies[c].start()

        def o_relay(z, way, c, onward):
            o_copy(z, way).copies[c].wait_recv()
            pl.when(onward)(lambda: o_copy(z, way).copies[c].start())
            o_copy(z, 2).copies[c].start()

        def from_partner(z):
            p = (1 - sec) * ncol + z
            piece_copy(anc_ref, p, 2).wait_recv()
            o_copy(z, 2).wait_recv()
            halves(anc.at[p], p)

        def early_step(t, carry):
            left = jnp.logical_and(col - t >= 0, early(sec, col - t))
            right = jnp.logical_and(col + t < ncol, early(sec, col + t))
            for c in range(CHUNKS):
                pl.when(left)(lambda: relay(mine - t, 1, c, col < ncol - 1))
                pl.when(right)(lambda: relay(mine + t, 0, c, col > 0))
            for c in range(OCHUNKS):
                pl.when(left)(lambda: o_relay(col - t, 1, c, col < ncol - 1))
                pl.when(right)(lambda: o_relay(col + t, 0, c, col > 0))
            pl.when(left)(lambda: halves(anc.at[mine - t], mine - t))
            pl.when(right)(lambda: halves(anc.at[mine + t], mine + t))
            left = jnp.logical_and(col - t >= 0, early(1 - sec, col - t))
            right = jnp.logical_and(col + t < ncol, early(1 - sec, col + t))
            pl.when(left)(lambda: from_partner(col - t))
            pl.when(right)(lambda: from_partner(col + t))
            return carry

        def spot(z):
            k = z % per
            return jnp.where(jnp.logical_or(native(z) == 1, sec == 1), k, 1 - k)

        def place(z):
            k = z % per
            seen = native(z)
            turned = seen == sec
            rpos = jnp.where(jnp.logical_or(seen == 1, sec == 0), k, 1 - k)
            here = pl.ds(pl.multiple_of(rpos * half, half), half)

            def put(value):
                high, low = split(value)
                oh[0, 0, spot(z), here] = high
                ol[0, 0, spot(z), here] = low

            pl.when(turned)(lambda: put(obuf[z].T))
            pl.when(jnp.logical_not(turned))(lambda: put(obuf[z]))

        def late_partner(p):
            piece_copy(anc_ref, p, 2).wait_recv()
            halves(anc.at[p], p)

        def late_step(t, ends):
            def wanted(p, z):
                edge = jnp.logical_or(z == 0, z == ncol - 1)
                return jnp.logical_and(late(p), edge if ends else jnp.logical_not(edge))

            left = jnp.logical_and(col - t >= 0, wanted(mine - t, col - t))
            right = jnp.logical_and(col + t < ncol, wanted(mine + t, col + t))
            for c in range(CHUNKS):
                pl.when(left)(lambda: relay(mine - t, 1, c, col < ncol - 1))
                pl.when(right)(lambda: relay(mine + t, 0, c, col > 0))
            pl.when(left)(lambda: halves(anc.at[mine - t], mine - t))
            pl.when(right)(lambda: halves(anc.at[mine + t], mine + t))

        def late_partners(t):
            left = jnp.logical_and(col - t >= 0, late(other - t))
            right = jnp.logical_and(col + t < ncol, late(other + t))
            pl.when(left)(lambda: late_partner(other - t))
            pl.when(right)(lambda: late_partner(other + t))

    else:
        @pl.when(jnp.logical_not(late(mine)))
        def _():
            send_mine()
            pass_on(anc_ref, mine)

        panels_out()
        settle_own()

        def settle(p):
            pass_on(anc.at[p], p)
            halves(anc.at[p], p)

        def from_partner(p):
            piece_copy(anc_ref, p, 2).wait_recv()
            pass_on(anc.at[p], p)
            halves(anc.at[p], p)

        def gather(phase):
            def ready(p):
                return late(p) if phase else jnp.logical_not(late(p))

            def step(t, carry):
                left = jnp.logical_and(col - t >= 0, ready(mine - t))
                right = jnp.logical_and(col + t < ncol, ready(mine + t))
                for c in range(CHUNKS):
                    pl.when(left)(lambda: relay(mine - t, 1, c, col < ncol - 1))
                    pl.when(right)(lambda: relay(mine + t, 0, c, col > 0))
                pl.when(left)(lambda: settle(mine - t))
                pl.when(right)(lambda: settle(mine + t))
                partners(t)
                return carry

            def partners(t):
                left = jnp.logical_and(col - t >= 0, ready(other - t))
                right = jnp.logical_and(col + t < ncol, ready(other + t))
                pl.when(left)(lambda: from_partner(other - t))
                pl.when(jnp.logical_and(right, t > 0))(lambda: from_partner(other + t))

            partners(0)
            lax.fori_loop(1, ncol, step, 0)

        gather(0)
        pl.when(late(mine))(send_mine)
        for d in range(1, nf):
            for e in range(1, ns):
                for k in range(per):
                    opp_copy(anc_ref, d, e, k).wait_recv()
                    high, low = split(opp[d - 1, e - 1, k])
                    oh[d - 1, e - 1, k] = high
                    ol[d - 1, e - 1, k] = low

    def q_copy(e, k, j, h):
        rr = pl.ds(j * SW + h * tm, tm)
        return copy(
            qsend.at[e - 1, k, rr], qrecv.at[e - 1, k, rr], qs.at[e - 1, k, j, h], qr.at[e - 1, k, j, h],
            {"row": at(f, (s + e) % ns)},
        )

    def products(k, fresh):
        for j in range(slots):
            for h in range(parts):
                rr = pl.ds(j * SW + h * tm, tm)
                for d in range(1, nf):
                    if fresh:
                        panel_copy(d, j, h).wait_recv()
                        keep(lambda i, cols: pin[d - 1, j, pl.ds(i * B, B), cols], j, h, d, at((f + nf - d) % nf, s))
                for e in range(1, ns):
                    p = at(f, (s + e) % ns) * per + k
                    acc = dot3(ph[0, rr], plo[0, rr], ah[p], al[p], NN)
                    for d in range(1, nf):
                        acc += dot3(ph[d, rr], plo[d, rr], oh[d - 1, e - 1, k], ol[d - 1, e - 1, k], NN)
                    qsend[e - 1, k, rr] = acc
                    q_copy(e, k, j, h).start()

    if crossed is not None:
        last = ncol - 1 - col
        pl.when(early(1 - sec, col))(lambda: from_partner(col))
        lax.fori_loop(1, ncol - 1, early_step, 0)
        pl.when(jnp.logical_and(late(mine), jnp.logical_not(at_end)))(send_mine)
        late_step(1, True)
        for z in range(ncol):
            pl.when(z != last)(functools.partial(place, z))
        products(1 - spot(last), True)
        early_step(ncol - 1, 0)
        place(last)
        products(spot(last), False)
        late_step(1, False)
    else:
        for k in range(per):
            products(k, k == 0)

    def near(i, carry):
        rr = pl.ds(pl.multiple_of(i * tm, tm), tm)
        acc = jnp.zeros((tm, width), F32)
        for d in range(1, nf):
            for k in range(per):
                p = at((f + nf - d) % nf, s) * per + k
                cols = pl.ds(k * pw, pw)
                acc += dot3(ph[d, rr, cols], plo[d, rr, cols], ah[p], al[p], NT)
        prod_ref[rr] = acc
        return carry

    lax.fori_loop(0, rows // tm, near, 0)
    if crossed is not None:
        pl.when(late(other))(lambda: late_partner(other))
        late_partners(1)
        for t in range(2, ncol):
            late_step(t, True)
            late_step(t, False)
            late_partners(t)
    else:
        gather(1)

    def own(i, carry):
        rr = pl.ds(pl.multiple_of(i * tm, tm), tm)
        for k in range(per):
            p = row * per + k
            prod_ref[rr, pl.ds(k * pw, pw)] += dot3(ph[0, rr], plo[0, rr], ah[p], al[p], NN)
        return carry

    lax.fori_loop(0, rows // tm, own, 0)

    span = nf * part

    def portion(i):
        return pl.ds(pl.multiple_of(i * span, 8), span)

    def across(d):
        return {"row": at(f, (s + d) % ns)}

    def along(d):
        return {"row": at((f + d) % nf, s)}

    def u_copy(j, d):
        return copy(
            upack.at[j, portion((s + d) % ns)], urecv.at[j, d - 1], us.at[j, d - 1], ur.at[j, d - 1], across(d)
        )

    def v_copy(j, d):
        return copy(
            usum.at[j, pl.ds(pl.multiple_of(((f + d) % nf) * part, 8), part)],
            urecv2.at[j, d - 1], us2.at[j, d - 1], ur2.at[j, d - 1], along(d),
        )

    def h_copy(j, d):
        done = pl.ds(pl.multiple_of((s * nf + f) * part, 8), part)
        return copy(ufin.at[j, done], ufin.at[j, done], gs2.at[j, d - 1], gr2.at[j, d - 1], along(d))

    def g_copy(j, d):
        return copy(ufin.at[j, portion(s)], ufin.at[j, portion(s)], gs.at[j, d - 1], gr.at[j, d - 1], across(d))

    ri = lax.broadcasted_iota(jnp.int32, (B, B), 0)
    ci = lax.broadcasted_iota(jnp.int32, (B, B), 1)
    rows8 = lax.broadcasted_iota(jnp.int32, (8, B), 0)
    offs, tail = spots(wb)

    def update_out(j):
        for h in range(parts):
            rr = pl.ds(j * SW + h * tm, tm)
            for e in range(1, ns):
                for k in range(per):
                    q_copy(e, k, j, h).wait_recv()
                    prod_ref[rr, pl.ds(k * pw, pw)] += qrecv[e - 1, k, rr]
        extra = jnp.zeros((8, B), F32)
        held = None
        for i in range(wb):
            qh, ql = split(prod_ref[pl.ds(j * SW + i * B, B)])
            rest = pl.ds(j * SW + i * B, SW - i * B)
            line = dot3(qh, ql, ph[0, rest], plo[0, rest], NT)
            for k in range(i + 1, wb):
                upack[j, pl.ds(offs[i, k], B)] = line[:, (k - i) * B:(k - i + 1) * B]
            if i % 2 == 0:
                held = line[:, :B]
            else:
                low = line[:, :B]
                upack[j, pl.ds(i // 2 * B, B)] = jnp.where(ri <= ci, held, low)
                mid = jnp.sum(jnp.where(ri == ci, low, 0.0), axis=0, keepdims=True)
                extra = jnp.where(rows8 == i // 2, mid, extra)
        upack[j, pl.ds(tail, 8)] = extra
        upack[j, pl.ds(tail + 8, 8 * (nrow - 1))] = jnp.zeros((8 * (nrow - 1), B), F32)
        for d in range(1, ns):
            u_copy(j, d).start()

    def second(j):
        for d in range(1, ns):
            u_copy(j, d).wait_recv()
        total = upack[j, portion(s)]
        for d in range(1, ns):
            total += urecv[j, d - 1]
        usum[j] = total
        for d in range(1, nf):
            v_copy(j, d).start()

    def third(j):
        for d in range(1, nf):
            v_copy(j, d).wait_recv()
        total = usum[j, pl.ds(pl.multiple_of(f * part, 8), part)]
        for d in range(1, nf):
            total += urecv2[j, d - 1]
        ufin[j, pl.ds(pl.multiple_of((s * nf + f) * part, 8), part)] = total
        for d in range(1, nf):
            h_copy(j, d).start()

    def fourth(j):
        for d in range(1, nf):
            h_copy(j, d).wait_recv()
        for d in range(1, ns):
            g_copy(j, d).start()

    def finish(j):
        for d in range(1, ns):
            g_copy(j, d).wait_recv()
        sum_ref[j] = ufin[j]

    stages = [update_out, second, third, fourth]
    for step in range(2 * (slots - 1) + len(stages)):
        for j in range(slots):
            if 0 <= step - 2 * j < len(stages):
                stages[step - 2 * j](j)
    for j in range(slots):
        finish(j)

    for j in range(slots):
        for d in range(1, ns):
            u_copy(j, d).wait_send()
            g_copy(j, d).wait_send()
        for d in range(1, nf):
            v_copy(j, d).wait_send()
            h_copy(j, d).wait_send()
        for h in range(parts):
            for e in range(1, ns):
                for k in range(per):
                    q_copy(e, k, j, h).wait_send()
            for d in range(1, nf):
                panel_copy(d, j, h).wait_send()

    if crossed is None:
        for d in range(1, nf):
            for e in range(1, ns):
                for k in range(per):
                    opp_copy(anc_ref, d, e, k).wait_send()

    def drain(q, carry):
        p = sec * ncol + q
        to_right = jnp.logical_and(q <= col, col < ncol - 1)
        to_left = jnp.logical_and(q >= col, col > 0)
        if crossed is None:
            sent = q >= 0
        else:
            sent = jnp.logical_or(early(sec, q), late(p))
        pl.when(jnp.logical_and(sent, to_right))(lambda: piece_copy(anc_ref, p, 1).wait_send())
        pl.when(jnp.logical_and(sent, to_left))(lambda: piece_copy(anc_ref, p, 0).wait_send())
        pl.when(sent)(lambda: piece_copy(anc_ref, p, 2).wait_send())
        if crossed is not None:
            first_half = early(sec, q)
            pl.when(jnp.logical_and(first_half, to_right))(lambda: o_copy(q, 1).wait_send())
            pl.when(jnp.logical_and(first_half, to_left))(lambda: o_copy(q, 0).wait_send())
            pl.when(first_half)(lambda: o_copy(q, 2).wait_send())
        return carry

    lax.fori_loop(0, ncol, drain, 0)
    if crossed is not None:
        @pl.when(is_opp)
        def _():
            cross_copies(0).wait_send()
            cross_copies(1).wait_send()


def write_out(ncol, parts, prod_ref, sum_ref, diag_ref, widths_ref, pattern_ref, off_ref, upd_ref):
    j, h = pl.program_id(0), pl.program_id(1)
    sec, row, col = lax.axis_index("sec"), lax.axis_index("row"), lax.axis_index("col")
    child = (sec * ncol + col) * pl.num_programs(0) + j
    wb = SW // B
    each = wb // parts
    blocks = off_ref.shape[1] // B
    offs, tail = spots(wb)
    ri = lax.broadcasted_iota(jnp.int32, (B, B), 0)
    ci = lax.broadcasted_iota(jnp.int32, (B, B), 1)
    fill = widths_ref[child]

    def inside(i):
        return jnp.where(fill > i, 1.0, 0.0).astype(F32)

    for i in range(each):
        here = pl.ds(i * B, B)
        for c in range(blocks):
            cols = pl.ds(c * B, B)
            present = pattern_ref[child, row * blocks + c].astype(F32)
            off_ref[here, cols] = prod_ref[here, cols] * -(inside(h * each + i) * present)

    def block_of(i, k):
        if i < k:
            return sum_ref[0, pl.ds(offs[i, k], B)]
        if i > k:
            return sum_ref[0, pl.ds(offs[k, i], B)].T
        both = sum_ref[0, pl.ds(i // 2 * B, B)]
        if i % 2 == 0:
            return jnp.where(ri <= ci, both, both.T)
        return jnp.where(ri == ci, sum_ref[0, pl.ds(tail + i // 2, 1)], jnp.where(ri > ci, both, both.T))

    for part in range(parts):
        @pl.when(h == part)
        def _():
            for i in range(each):
                for k in range(wb):
                    here = (pl.ds(i * B, B), pl.ds(k * B, B))
                    upd_ref[here] = (diag_ref[here] + block_of(part * each + i, k)) * inside(max(part * each + i, k))


def local(sizes, anc_inverse, panel, diag_inverse, widths, pattern):
    nsec, nrow, ncol, nf, ns, nb, square = sizes
    rows, width = panel.shape
    pw = anc_inverse.shape[1]
    per = width // pw
    slots = rows // SW
    pieces = nsec * ncol
    packed = packed_rows(nrow)
    part = packed // nrow
    parts = SW // TM
    short = square and nsec == nb == per == 2 and ncol == per * nb
    vm = pltpu.VMEM
    dma = pltpu.SemaphoreType.DMA
    whole = pl.BlockSpec(memory_space=pltpu.VMEM)
    scalar = pl.BlockSpec(memory_space=pltpu.SMEM)
    product, summed = pl.pallas_call(
        functools.partial(kernel, sizes),
        out_shape=(jax.ShapeDtypeStruct((rows, width), F32), jax.ShapeDtypeStruct((slots, packed, B), F32)),
        in_specs=[whole, whole, scalar, scalar],
        out_specs=(whole, whole),
        scratch_shapes=[
            vm((pieces, width, pw), F32),
            vm((pieces, width, pw), BF),
            vm((pieces, width, pw), BF),
            vm((nf, rows, width), BF),
            vm((nf, rows, width), BF),
            vm((nf - 1, slots, SW, width), F32),
            None if short else vm((nf - 1, ns - 1, per, width, pw), F32),
            vm((nf - 1, ns - 1, per, width, pw), BF),
            vm((nf - 1, ns - 1, per, width, pw), BF),
            vm((ns - 1, per, rows, pw), F32),
            vm((ns - 1, per, rows, pw), F32),
            vm((slots, packed, B), F32),
            vm((slots, ns - 1, nf * part, B), F32),
            vm((slots, nf * part, B), F32),
            vm((slots, nf - 1, part, B), F32),
            vm((slots, packed, B), F32),
            dma((pieces, 3, CHUNKS)), dma((pieces, CHUNKS)),
            dma((nf - 1, slots, parts)), dma((nf - 1, slots, parts)),
            None if short else dma((nf - 1, ns - 1, per)), None if short else dma((nf - 1, ns - 1, per)),
            dma((ns - 1, per, slots, parts)), dma((ns - 1, per, slots, parts)),
            dma((slots, ns - 1)), dma((slots, ns - 1)),
            dma((slots, nf - 1)), dma((slots, nf - 1)),
            dma((slots, nf - 1)), dma((slots, nf - 1)),
            dma((slots, ns - 1)), dma((slots, ns - 1)),
            (
                vm((ncol, width // 2, pw), F32), dma((2, OCHUNKS)), dma((OCHUNKS,)),
                dma((ncol, 3, OCHUNKS)), dma((ncol, OCHUNKS)),
            ) if short else None,
        ],
        compiler_params=pltpu.CompilerParams(
            collective_id=0, has_side_effects=True, vmem_limit_bytes=(40 if short else 60) * 1024 * 1024
        ),
    )(anc_inverse, panel, widths, pattern)
    strip = pl.BlockSpec((TM, width), lambda j, h: (j * parts + h, 0))
    square_strip = pl.BlockSpec((TM, SW), lambda j, h: (j * parts + h, 0))
    return pl.pallas_call(
        functools.partial(write_out, ncol, parts),
        grid=(slots, parts),
        out_shape=(jax.ShapeDtypeStruct((rows, width), F32), jax.ShapeDtypeStruct((rows, SW), F32)),
        in_specs=[strip, pl.BlockSpec((1, packed, B), lambda j, h: (j, 0, 0)), square_strip, scalar, scalar],
        out_specs=(strip, square_strip),
        compiler_params=pltpu.CompilerParams(vmem_limit_bytes=16 * 1024 * 1024),
    )(product, summed, diag_inverse, widths, pattern)


def solution(mesh):
    shape = dict(mesh.shape)
    na, nb = factor(shape["row"])
    sizes = (shape["sec"], shape["row"], shape["col"], na, nb, nb, na == nb)
    in_specs = (
        P("row", ("sec", "col")),
        P(("sec", "col"), "row"),
        P(("sec", "col"), None),
        P(),
        P(),
    )
    out_specs = (P(("sec", "col"), "row"), P(("sec", "col"), None))
    return jax.shard_map(
        functools.partial(local, sizes), mesh=mesh, in_specs=in_specs, out_specs=out_specs, check_vma=False
    )
```

```python
import functools
import jax
import jax.numpy as jnp
from jax import lax
from jax.experimental import pallas as pl
from jax.experimental.pallas import tpu as pltpu
from jax.sharding import PartitionSpec as P

B = 128
SW = 512
CHUNKS = 8
OCHUNKS = 4
TM = 256
F32 = jnp.float32
BF = jnp.bfloat16
MESH = pl.DeviceIdType.MESH
NN = (((1,), (0,)), ((), ()))
NT = (((1,), (1,)), ((), ()))


def split(value):
    high = value.astype(BF)
    return high, (value - high.astype(F32)).astype(BF)


def dot3(ah, al, bh, bl, dims):
    dot = functools.partial(lax.dot_general, dimension_numbers=dims, preferred_element_type=F32)
    return dot(ah, bh) + (dot(ah, bl) + dot(al, bh))


def packed_rows(nrow):
    wb = SW // B
    return (wb * (wb + 1) // 2 - wb // 2) * B + 8 * nrow


def spots(wb):
    offs = {}
    for i in range(wb):
        for k in range(i + 1, wb):
            offs[i, k] = (wb // 2 + len(offs)) * B
    return offs, (wb // 2 + len(offs)) * B


def factor(count):
    low = 1
    for value in range(1, count + 1):
        if count % value == 0 and value * value <= count:
            low = value
    return count // low, low


class Group:
    def __init__(self, copies):
        self.copies = copies

    def start(self):
        for one in self.copies:
            one.start()

    def wait_recv(self):
        for one in self.copies:
            one.wait_recv()

    def wait_send(self):
        for one in self.copies:
            one.wait_send()


def kernel(
    sizes,
    anc_ref, panel_ref, widths_ref, pattern_ref, prod_ref, sum_ref,
    anc, ah, al, ph, plo, pin, opp, oh, ol, qsend, qrecv, upack, urecv, usum, urecv2, ufin,
    zs, zr, ps, pr, os_, or_, qs, qr, us, ur, us2, ur2, gs2, gr2, gs, gr, anc_own, panel_own, fills, fits, ds, crossed,
):
    nsec, nrow, ncol, nf, ns, nb, square = sizes
    rows, width = panel_ref.shape
    pw = anc_ref.shape[1]
    per = width // pw
    slots = rows // SW
    wb = SW // B
    part = packed_rows(nrow) // nrow
    tm = TM
    parts = SW // tm
    sec, row, col = lax.axis_index("sec"), lax.axis_index("row"), lax.axis_index("col")
    turn = sec if square else 0
    a, b = row // nb, row % nb
    f = a + turn * (b - a)
    s = b + turn * (a - b)
    cf = nb - turn * (nb - 1)
    cs = 1 + turn * (nb - 1)

    def at(fi, si):
        return fi * cf + si * cs

    def copy(src, dst, send, recv, where):
        return pltpu.make_async_remote_copy(
            src_ref=src, dst_ref=dst, send_sem=send, recv_sem=recv, device_id=where, device_id_type=MESH
        )

    loads = [
        pltpu.make_async_copy(source, target, ds.at[i])
        for i, (source, target) in enumerate(
            ((widths_ref, fills), (pattern_ref, fits), (anc_ref, anc_own), (panel_ref, panel_own))
        )
    ]
    for one in loads:
        one.start()

    first = (sec * ncol + col) * slots
    blocks = width // B

    def inside(j, i):
        return jnp.where(fills[first + j] > i, 1.0, 0.0).astype(F32)

    def present(j, r, c):
        return fits[first + j, r * blocks + c].astype(F32)

    def keep(src, j, h, slot, r):
        for i in range(h * wb // parts, (h + 1) * wb // parts):
            here = pl.ds(j * SW + i * B, B)
            for c in range(blocks):
                cols = pl.ds(c * B, B)
                high, low = split(src(i, cols) * (inside(j, i) * present(j, r, c)))
                ph[slot, here, cols] = high
                plo[slot, here, cols] = low

    has_left = (col > 0).astype(jnp.int32)
    has_right = (col < ncol - 1).astype(jnp.int32)
    barrier = pltpu.get_barrier_semaphore()
    for d in range(1, nrow):
        pl.semaphore_signal(barrier, inc=1, device_id={"row": (row + d) % nrow}, device_id_type=MESH)
    pl.semaphore_signal(barrier, inc=1, device_id={"sec": 1 - sec}, device_id_type=MESH)

    @pl.when(col > 0)
    def _():
        pl.semaphore_signal(barrier, inc=1, device_id={"col": col - 1}, device_id_type=MESH)

    @pl.when(col < ncol - 1)
    def _():
        pl.semaphore_signal(barrier, inc=1, device_id={"col": col + 1}, device_id_type=MESH)

    pl.semaphore_wait(barrier, nrow + has_left + has_right)

    mine = sec * ncol + col

    def piece_copy(src, p, way):
        where = ({"col": col - 1}, {"col": col + 1}, {"sec": 1 - sec})[way]
        size = src.shape[0] // CHUNKS
        return Group([
            copy(
                src.at[pl.ds(c * size, size)], anc.at[p, pl.ds(c * size, size)],
                zs.at[p, way, c], zr.at[p, c], where,
            )
            for c in range(CHUNKS)
        ])

    def opp_copy(src, d, e, k):
        return copy(
            src, opp.at[d - 1, e - 1, k], os_.at[d - 1, e - 1, k], or_.at[d - 1, e - 1, k],
            {"row": at((f + d) % nf, s)},
        )

    def pass_on(src, p):
        for d in range(1, nf):
            for e in range(1, ns):
                @pl.when(p // per == at((f + d) % nf, (s + e) % ns))
                def _():
                    opp_copy(src, d, e, p % per).start()

    def panel_copy(d, j, h):
        return copy(
            panel_ref.at[pl.ds(j * SW + h * tm, tm)], pin.at[d - 1, j, pl.ds(h * tm, tm)],
            ps.at[d - 1, j, h], pr.at[d - 1, j, h], {"row": at((f + d) % nf, s)},
        )

    def halves(src, p):
        high, low = split(src[...])
        ah[p] = high
        al[p] = low

    def late(p):
        return p // per == row

    def send_mine():
        pl.when(col > 0)(lambda: piece_copy(anc_ref, mine, 0).start())
        pl.when(col < ncol - 1)(lambda: piece_copy(anc_ref, mine, 1).start())
        piece_copy(anc_ref, mine, 2).start()

    other = (1 - sec) * ncol + col

    def panels_out():
        for j in range(slots):
            for h in range(parts):
                for d in range(1, nf):
                    panel_copy(d, j, h).start()

    def settle_own():
        for one in loads:
            one.wait()
        halves(anc_own, mine)
        for j in range(slots):
            for h in range(parts):
                keep(lambda i, cols: panel_own[pl.ds(j * SW + i * B, B), cols], j, h, 0, row)

    def relay(p, way, c, onward):
        piece_copy(anc_ref, p, way).copies[c].wait_recv()
        pl.when(onward)(lambda: piece_copy(anc.at[p], p, way).copies[c].start())
        piece_copy(anc.at[p], p, 2).copies[c].start()

    if crossed is not None:
        obuf, xs, xr, zos, zor = crossed
        half = width // 2
        osize = half // OCHUNKS

        def native(z):
            return (z // per != b).astype(jnp.int32)

        def early(side, z):
            return native(z) == (side == a).astype(jnp.int32)

        def cross_copies(axis):
            where = {"row": (1 - a) * nb + b} if axis == 0 else {"row": a * nb + 1 - b}
            k = col % per
            base = (k if axis == 0 else 1 - k) * half
            return Group([
                copy(
                    anc_ref.at[pl.ds(pl.multiple_of(base + c * osize, 8), osize)],
                    obuf.at[col, pl.ds(c * osize, osize)], xs.at[axis, c], xr.at[c], where,
                )
                for c in range(OCHUNKS)
            ])

        def o_copy(z, way):
            where = ({"col": col - 1}, {"col": col + 1}, {"sec": 1 - sec})[way]
            return Group([
                copy(
                    obuf.at[z, pl.ds(c * osize, osize)], obuf.at[z, pl.ds(c * osize, osize)],
                    zos.at[z, way, c], zor.at[z, c], where,
                )
                for c in range(OCHUNKS)
            ])

        is_early = early(sec, col)
        is_opp = jnp.logical_and(native(col) == 1, sec != a)

        @pl.when(is_opp)
        def _():
            cross_copies(0).start()
            cross_copies(1).start()

        at_end = jnp.logical_or(col == 0, col == ncol - 1)
        pl.when(is_early)(send_mine)
        panels_out()
        pl.when(jnp.logical_and(late(mine), at_end))(send_mine)
        settle_own()

        @pl.when(is_early)
        def _():
            for c in range(OCHUNKS):
                cross_copies(0).copies[c].wait_recv()
                pl.when(col > 0)(lambda: o_copy(col, 0).copies[c].start())
                pl.when(col < ncol - 1)(lambda: o_copy(col, 1).copies[c].start())
                o_copy(col, 2).copies[c].start()

        def o_relay(z, way, c, onward):
            o_copy(z, way).copies[c].wait_recv()
            pl.when(onward)(lambda: o_copy(z, way).copies[c].start())
            o_copy(z, 2).copies[c].start()

        def from_partner(z):
            p = (1 - sec) * ncol + z
            piece_copy(anc_ref, p, 2).wait_recv()
            o_copy(z, 2).wait_recv()
            halves(anc.at[p], p)

        def early_step(t, carry):
            left = jnp.logical_and(col - t >= 0, early(sec, col - t))
            right = jnp.logical_and(col + t < ncol, early(sec, col + t))
            for c in range(CHUNKS):
                pl.when(left)(lambda: relay(mine - t, 1, c, col < ncol - 1))
                pl.when(right)(lambda: relay(mine + t, 0, c, col > 0))
            for c in range(OCHUNKS):
                pl.when(left)(lambda: o_relay(col - t, 1, c, col < ncol - 1))
                pl.when(right)(lambda: o_relay(col + t, 0, c, col > 0))
            pl.when(left)(lambda: halves(anc.at[mine - t], mine - t))
            pl.when(right)(lambda: halves(anc.at[mine + t], mine + t))
            left = jnp.logical_and(col - t >= 0, early(1 - sec, col - t))
            right = jnp.logical_and(col + t < ncol, early(1 - sec, col + t))
            pl.when(left)(lambda: from_partner(col - t))
            pl.when(right)(lambda: from_partner(col + t))
            return carry

        def spot(z):
            k = z % per
            return jnp.where(jnp.logical_or(native(z) == 1, sec == 1), k, 1 - k)

        def place(z):
            k = z % per
            seen = native(z)
            turned = seen == sec
            rpos = jnp.where(jnp.logical_or(seen == 1, sec == 0), k, 1 - k)
            here = pl.ds(pl.multiple_of(rpos * half, half), half)

            def put(value):
                high, low = split(value)
                oh[0, 0, spot(z), here] = high
                ol[0, 0, spot(z), here] = low

            pl.when(turned)(lambda: put(obuf[z].T))
            pl.when(jnp.logical_not(turned))(lambda: put(obuf[z]))

        def late_partner(p):
            piece_copy(anc_ref, p, 2).wait_recv()
            halves(anc.at[p], p)

        def late_step(t, ends):
            def wanted(p, z):
                edge = jnp.logical_or(z == 0, z == ncol - 1)
                return jnp.logical_and(late(p), edge if ends else jnp.logical_not(edge))

            left = jnp.logical_and(col - t >= 0, wanted(mine - t, col - t))
            right = jnp.logical_and(col + t < ncol, wanted(mine + t, col + t))
            for c in range(CHUNKS):
                pl.when(left)(lambda: relay(mine - t, 1, c, col < ncol - 1))
                pl.when(right)(lambda: relay(mine + t, 0, c, col > 0))
            pl.when(left)(lambda: halves(anc.at[mine - t], mine - t))
            pl.when(right)(lambda: halves(anc.at[mine + t], mine + t))

        def late_partners(t):
            left = jnp.logical_and(col - t >= 0, late(other - t))
            right = jnp.logical_and(col + t < ncol, late(other + t))
            pl.when(left)(lambda: late_partner(other - t))
            pl.when(right)(lambda: late_partner(other + t))

    else:
        @pl.when(jnp.logical_not(late(mine)))
        def _():
            send_mine()
            pass_on(anc_ref, mine)

        panels_out()
        settle_own()

        def settle(p):
            pass_on(anc.at[p], p)
            halves(anc.at[p], p)

        def from_partner(p):
            piece_copy(anc_ref, p, 2).wait_recv()
            pass_on(anc.at[p], p)
            halves(anc.at[p], p)

        def gather(phase):
            def ready(p):
                return late(p) if phase else jnp.logical_not(late(p))

            def step(t, carry):
                left = jnp.logical_and(col - t >= 0, ready(mine - t))
                right = jnp.logical_and(col + t < ncol, ready(mine + t))
                for c in range(CHUNKS):
                    pl.when(left)(lambda: relay(mine - t, 1, c, col < ncol - 1))
                    pl.when(right)(lambda: relay(mine + t, 0, c, col > 0))
                pl.when(left)(lambda: settle(mine - t))
                pl.when(right)(lambda: settle(mine + t))
                partners(t)
                return carry

            def partners(t):
                left = jnp.logical_and(col - t >= 0, ready(other - t))
                right = jnp.logical_and(col + t < ncol, ready(other + t))
                pl.when(left)(lambda: from_partner(other - t))
                pl.when(jnp.logical_and(right, t > 0))(lambda: from_partner(other + t))

            partners(0)
            lax.fori_loop(1, ncol, step, 0)

        gather(0)
        pl.when(late(mine))(send_mine)
        for d in range(1, nf):
            for e in range(1, ns):
                for k in range(per):
                    opp_copy(anc_ref, d, e, k).wait_recv()
                    high, low = split(opp[d - 1, e - 1, k])
                    oh[d - 1, e - 1, k] = high
                    ol[d - 1, e - 1, k] = low

    def q_copy(e, k, j, h):
        rr = pl.ds(j * SW + h * tm, tm)
        return copy(
            qsend.at[e - 1, k, rr], qrecv.at[e - 1, k, rr], qs.at[e - 1, k, j, h], qr.at[e - 1, k, j, h],
            {"row": at(f, (s + e) % ns)},
        )

    def products(k, fresh):
        for j in range(slots):
            for h in range(parts):
                rr = pl.ds(j * SW + h * tm, tm)
                for d in range(1, nf):
                    if fresh:
                        panel_copy(d, j, h).wait_recv()
                        keep(lambda i, cols: pin[d - 1, j, pl.ds(i * B, B), cols], j, h, d, at((f + nf - d) % nf, s))
                for e in range(1, ns):
                    p = at(f, (s + e) % ns) * per + k
                    acc = dot3(ph[0, rr], plo[0, rr], ah[p], al[p], NN)
                    for d in range(1, nf):
                        acc += dot3(ph[d, rr], plo[d, rr], oh[d - 1, e - 1, k], ol[d - 1, e - 1, k], NN)
                    qsend[e - 1, k, rr] = acc
                    q_copy(e, k, j, h).start()

    if crossed is not None:
        last = ncol - 1 - col
        pl.when(early(1 - sec, col))(lambda: from_partner(col))
        lax.fori_loop(1, ncol - 1, early_step, 0)
        pl.when(jnp.logical_and(late(mine), jnp.logical_not(at_end)))(send_mine)
        late_step(1, True)
        for z in range(ncol):
            pl.when(z != last)(functools.partial(place, z))
        products(1 - spot(last), True)
        late_step(1, False)
        late_step(2, True)
        early_step(ncol - 1, 0)
        place(last)
        products(spot(last), False)
        late_step(2, False)
    else:
        for k in range(per):
            products(k, k == 0)

    def near(i, carry):
        rr = pl.ds(pl.multiple_of(i * tm, tm), tm)
        acc = jnp.zeros((tm, width), F32)
        for d in range(1, nf):
            for k in range(per):
                p = at((f + nf - d) % nf, s) * per + k
                cols = pl.ds(k * pw, pw)
                acc += dot3(ph[d, rr, cols], plo[d, rr, cols], ah[p], al[p], NT)
        prod_ref[rr] = acc
        return carry

    lax.fori_loop(0, rows // tm, near, 0)
    if crossed is not None:
        pl.when(late(other))(lambda: late_partner(other))
        for t in range(1, ncol):
            if t > 2:
                late_step(t, True)
                late_step(t, False)
            late_partners(t)
    else:
        gather(1)

    def own(i, carry):
        rr = pl.ds(pl.multiple_of(i * tm, tm), tm)
        for k in range(per):
            p = row * per + k
            prod_ref[rr, pl.ds(k * pw, pw)] += dot3(ph[0, rr], plo[0, rr], ah[p], al[p], NN)
        return carry

    lax.fori_loop(0, rows // tm, own, 0)

    span = nf * part

    def portion(i):
        return pl.ds(pl.multiple_of(i * span, 8), span)

    def across(d):
        return {"row": at(f, (s + d) % ns)}

    def along(d):
        return {"row": at((f + d) % nf, s)}

    def u_copy(j, d):
        return copy(
            upack.at[j, portion((s + d) % ns)], urecv.at[j, d - 1], us.at[j, d - 1], ur.at[j, d - 1], across(d)
        )

    def v_copy(j, d):
        return copy(
            usum.at[j, pl.ds(pl.multiple_of(((f + d) % nf) * part, 8), part)],
            urecv2.at[j, d - 1], us2.at[j, d - 1], ur2.at[j, d - 1], along(d),
        )

    def h_copy(j, d):
        done = pl.ds(pl.multiple_of((s * nf + f) * part, 8), part)
        return copy(ufin.at[j, done], ufin.at[j, done], gs2.at[j, d - 1], gr2.at[j, d - 1], along(d))

    def g_copy(j, d):
        return copy(ufin.at[j, portion(s)], ufin.at[j, portion(s)], gs.at[j, d - 1], gr.at[j, d - 1], across(d))

    ri = lax.broadcasted_iota(jnp.int32, (B, B), 0)
    ci = lax.broadcasted_iota(jnp.int32, (B, B), 1)
    rows8 = lax.broadcasted_iota(jnp.int32, (8, B), 0)
    offs, tail = spots(wb)

    def update_out(j):
        for h in range(parts):
            rr = pl.ds(j * SW + h * tm, tm)
            for e in range(1, ns):
                for k in range(per):
                    q_copy(e, k, j, h).wait_recv()
                    prod_ref[rr, pl.ds(k * pw, pw)] += qrecv[e - 1, k, rr]
        extra = jnp.zeros((8, B), F32)
        held = None
        for i in range(wb):
            qh, ql = split(prod_ref[pl.ds(j * SW + i * B, B)])
            rest = pl.ds(j * SW + i * B, SW - i * B)
            line = dot3(qh, ql, ph[0, rest], plo[0, rest], NT)
            for k in range(i + 1, wb):
                upack[j, pl.ds(offs[i, k], B)] = line[:, (k - i) * B:(k - i + 1) * B]
            if i % 2 == 0:
                held = line[:, :B]
            else:
                low = line[:, :B]
                upack[j, pl.ds(i // 2 * B, B)] = jnp.where(ri <= ci, held, low)
                mid = jnp.sum(jnp.where(ri == ci, low, 0.0), axis=0, keepdims=True)
                extra = jnp.where(rows8 == i // 2, mid, extra)
        upack[j, pl.ds(tail, 8)] = extra
        upack[j, pl.ds(tail + 8, 8 * (nrow - 1))] = jnp.zeros((8 * (nrow - 1), B), F32)
        for d in range(1, ns):
            u_copy(j, d).start()

    def second(j):
        for d in range(1, ns):
            u_copy(j, d).wait_recv()
        total = upack[j, portion(s)]
        for d in range(1, ns):
            total += urecv[j, d - 1]
        usum[j] = total
        for d in range(1, nf):
            v_copy(j, d).start()

    def third(j):
        for d in range(1, nf):
            v_copy(j, d).wait_recv()
        total = usum[j, pl.ds(pl.multiple_of(f * part, 8), part)]
        for d in range(1, nf):
            total += urecv2[j, d - 1]
        ufin[j, pl.ds(pl.multiple_of((s * nf + f) * part, 8), part)] = total
        for d in range(1, nf):
            h_copy(j, d).start()

    def fourth(j):
        for d in range(1, nf):
            h_copy(j, d).wait_recv()
        for d in range(1, ns):
            g_copy(j, d).start()

    def finish(j):
        for d in range(1, ns):
            g_copy(j, d).wait_recv()
        sum_ref[j] = ufin[j]

    stages = [update_out, second, third, fourth]
    for step in range(slots - 1 + len(stages)):
        for j in reversed(range(slots)):
            if 0 <= step - j < len(stages):
                stages[step - j](j)
    for j in range(slots):
        finish(j)

    for j in range(slots):
        for d in range(1, ns):
            u_copy(j, d).wait_send()
            g_copy(j, d).wait_send()
        for d in range(1, nf):
            v_copy(j, d).wait_send()
            h_copy(j, d).wait_send()
        for h in range(parts):
            for e in range(1, ns):
                for k in range(per):
                    q_copy(e, k, j, h).wait_send()
            for d in range(1, nf):
                panel_copy(d, j, h).wait_send()

    if crossed is None:
        for d in range(1, nf):
            for e in range(1, ns):
                for k in range(per):
                    opp_copy(anc_ref, d, e, k).wait_send()

    def drain(q, carry):
        p = sec * ncol + q
        to_right = jnp.logical_and(q <= col, col < ncol - 1)
        to_left = jnp.logical_and(q >= col, col > 0)
        if crossed is None:
            sent = q >= 0
        else:
            sent = jnp.logical_or(early(sec, q), late(p))
        pl.when(jnp.logical_and(sent, to_right))(lambda: piece_copy(anc_ref, p, 1).wait_send())
        pl.when(jnp.logical_and(sent, to_left))(lambda: piece_copy(anc_ref, p, 0).wait_send())
        pl.when(sent)(lambda: piece_copy(anc_ref, p, 2).wait_send())
        if crossed is not None:
            first_half = early(sec, q)
            pl.when(jnp.logical_and(first_half, to_right))(lambda: o_copy(q, 1).wait_send())
            pl.when(jnp.logical_and(first_half, to_left))(lambda: o_copy(q, 0).wait_send())
            pl.when(first_half)(lambda: o_copy(q, 2).wait_send())
        return carry

    lax.fori_loop(0, ncol, drain, 0)
    if crossed is not None:
        @pl.when(is_opp)
        def _():
            cross_copies(0).wait_send()
            cross_copies(1).wait_send()


def write_out(ncol, parts, prod_ref, sum_ref, diag_ref, widths_ref, pattern_ref, off_ref, upd_ref):
    j, h = pl.program_id(0), pl.program_id(1)
    sec, row, col = lax.axis_index("sec"), lax.axis_index("row"), lax.axis_index("col")
    child = (sec * ncol + col) * pl.num_programs(0) + j
    wb = SW // B
    each = wb // parts
    blocks = off_ref.shape[1] // B
    offs, tail = spots(wb)
    ri = lax.broadcasted_iota(jnp.int32, (B, B), 0)
    ci = lax.broadcasted_iota(jnp.int32, (B, B), 1)
    fill = widths_ref[child]

    def inside(i):
        return jnp.where(fill > i, 1.0, 0.0).astype(F32)

    for i in range(each):
        here = pl.ds(i * B, B)
        for c in range(blocks):
            cols = pl.ds(c * B, B)
            present = pattern_ref[child, row * blocks + c].astype(F32)
            off_ref[here, cols] = prod_ref[here, cols] * -(inside(h * each + i) * present)

    def block_of(i, k):
        if i < k:
            return sum_ref[0, pl.ds(offs[i, k], B)]
        if i > k:
            return sum_ref[0, pl.ds(offs[k, i], B)].T
        both = sum_ref[0, pl.ds(i // 2 * B, B)]
        if i % 2 == 0:
            return jnp.where(ri <= ci, both, both.T)
        return jnp.where(ri == ci, sum_ref[0, pl.ds(tail + i // 2, 1)], jnp.where(ri > ci, both, both.T))

    for part in range(parts):
        @pl.when(h == part)
        def _():
            for i in range(each):
                for k in range(wb):
                    here = (pl.ds(i * B, B), pl.ds(k * B, B))
                    upd_ref[here] = (diag_ref[here] + block_of(part * each + i, k)) * inside(max(part * each + i, k))


def local(sizes, anc_inverse, panel, diag_inverse, widths, pattern):
    nsec, nrow, ncol, nf, ns, nb, square = sizes
    rows, width = panel.shape
    pw = anc_inverse.shape[1]
    per = width // pw
    slots = rows // SW
    pieces = nsec * ncol
    packed = packed_rows(nrow)
    part = packed // nrow
    parts = SW // TM
    short = square and nsec == nb == per == 2 and ncol == per * nb
    vm = pltpu.VMEM
    dma = pltpu.SemaphoreType.DMA
    whole = pl.BlockSpec(memory_space=pltpu.VMEM)
    scalar = pl.BlockSpec(memory_space=pltpu.SMEM)
    far = pl.BlockSpec(memory_space=pltpu.HBM)
    product, summed = pl.pallas_call(
        functools.partial(kernel, sizes),
        out_shape=(jax.ShapeDtypeStruct((rows, width), F32), jax.ShapeDtypeStruct((slots, packed, B), F32)),
        in_specs=[far, far, far, far],
        out_specs=(whole, whole),
        scratch_shapes=[
            vm((pieces, width, pw), F32),
            vm((pieces, width, pw), BF),
            vm((pieces, width, pw), BF),
            vm((nf, rows, width), BF),
            vm((nf, rows, width), BF),
            vm((nf - 1, slots, SW, width), F32),
            None if short else vm((nf - 1, ns - 1, per, width, pw), F32),
            vm((nf - 1, ns - 1, per, width, pw), BF),
            vm((nf - 1, ns - 1, per, width, pw), BF),
            vm((ns - 1, per, rows, pw), F32),
            vm((ns - 1, per, rows, pw), F32),
            vm((slots, packed, B), F32),
            vm((slots, ns - 1, nf * part, B), F32),
            vm((slots, nf * part, B), F32),
            vm((slots, nf - 1, part, B), F32),
            vm((slots, packed, B), F32),
            dma((pieces, 3, CHUNKS)), dma((pieces, CHUNKS)),
            dma((nf - 1, slots, parts)), dma((nf - 1, slots, parts)),
            None if short else dma((nf - 1, ns - 1, per)), None if short else dma((nf - 1, ns - 1, per)),
            dma((ns - 1, per, slots, parts)), dma((ns - 1, per, slots, parts)),
            dma((slots, ns - 1)), dma((slots, ns - 1)),
            dma((slots, nf - 1)), dma((slots, nf - 1)),
            dma((slots, nf - 1)), dma((slots, nf - 1)),
            dma((slots, ns - 1)), dma((slots, ns - 1)),
            vm((width, pw), F32), vm((rows, width), F32),
            pltpu.SMEM(widths.shape, widths.dtype), pltpu.SMEM(pattern.shape, pattern.dtype), dma((4,)),
            (
                vm((ncol, width // 2, pw), F32), dma((2, OCHUNKS)), dma((OCHUNKS,)),
                dma((ncol, 3, OCHUNKS)), dma((ncol, OCHUNKS)),
            ) if short else None,
        ],
        compiler_params=pltpu.CompilerParams(
            collective_id=0, has_side_effects=True, vmem_limit_bytes=(49 if short else 60) * 1024 * 1024
        ),
    )(anc_inverse, panel, widths, pattern)
    strip = pl.BlockSpec((TM, width), lambda j, h: (j * parts + h, 0))
    square_strip = pl.BlockSpec((TM, SW), lambda j, h: (j * parts + h, 0))
    return pl.pallas_call(
        functools.partial(write_out, ncol, parts),
        grid=(slots, parts),
        out_shape=(jax.ShapeDtypeStruct((rows, width), F32), jax.ShapeDtypeStruct((rows, SW), F32)),
        in_specs=[strip, pl.BlockSpec((1, packed, B), lambda j, h: (j, 0, 0)), square_strip, scalar, scalar],
        out_specs=(strip, square_strip),
        compiler_params=pltpu.CompilerParams(vmem_limit_bytes=16 * 1024 * 1024),
    )(product, summed, diag_inverse, widths, pattern)


def solution(mesh):
    shape = dict(mesh.shape)
    na, nb = factor(shape["row"])
    sizes = (shape["sec"], shape["row"], shape["col"], na, nb, nb, na == nb)
    in_specs = (
        P("row", ("sec", "col")),
        P(("sec", "col"), "row"),
        P(("sec", "col"), None),
        P(),
        P(),
    )
    out_specs = (P(("sec", "col"), "row"), P(("sec", "col"), None))
    return jax.shard_map(
        functools.partial(local, sizes), mesh=mesh, in_specs=in_specs, out_specs=out_specs, check_vma=False
    )
```

```python
import functools
import jax
import jax.numpy as jnp
from jax import lax
from jax.experimental import pallas as pl
from jax.experimental.pallas import tpu as pltpu
from jax.sharding import PartitionSpec as P

B = 128
SW = 512
CHUNKS = 8
OCHUNKS = 4
TM = 256
F32 = jnp.float32
BF = jnp.bfloat16
MESH = pl.DeviceIdType.MESH
NN = (((1,), (0,)), ((), ()))
NT = (((1,), (1,)), ((), ()))


def split(value):
    high = value.astype(BF)
    return high, (value - high.astype(F32)).astype(BF)


def dot3(ah, al, bh, bl, dims):
    dot = functools.partial(lax.dot_general, dimension_numbers=dims, preferred_element_type=F32)
    return dot(ah, bh) + (dot(ah, bl) + dot(al, bh))


def packed_rows(nrow):
    wb = SW // B
    return (wb * (wb + 1) // 2 - wb // 2) * B + 8 * nrow


def spots(wb):
    offs = {}
    for i in range(wb):
        for k in range(i + 1, wb):
            offs[i, k] = (wb // 2 + len(offs)) * B
    return offs, (wb // 2 + len(offs)) * B


def factor(count):
    low = 1
    for value in range(1, count + 1):
        if count % value == 0 and value * value <= count:
            low = value
    return count // low, low


class Group:
    def __init__(self, copies):
        self.copies = copies

    def start(self):
        for one in self.copies:
            one.start()

    def wait_recv(self):
        for one in self.copies:
            one.wait_recv()

    def wait_send(self):
        for one in self.copies:
            one.wait_send()


def kernel(
    sizes,
    anc_ref, panel_ref, widths_ref, pattern_ref, prod_ref, sum_ref,
    anc, ah, al, ph, plo, pin, opp, oh, ol, qsend, qrecv, upack, urecv, usum, urecv2, ufin,
    zs, zr, ps, pr, os_, or_, qs, qr, us, ur, us2, ur2, gs2, gr2, gs, gr, anc_own, panel_own, fills, fits, ds, crossed,
):
    nsec, nrow, ncol, nf, ns, nb, square = sizes
    rows, width = panel_ref.shape
    pw = anc_ref.shape[1]
    per = width // pw
    slots = rows // SW
    wb = SW // B
    part = packed_rows(nrow) // nrow
    tm = TM
    parts = SW // tm
    sec, row, col = lax.axis_index("sec"), lax.axis_index("row"), lax.axis_index("col")
    turn = sec if square else 0
    a, b = row // nb, row % nb
    f = a + turn * (b - a)
    s = b + turn * (a - b)
    cf = nb - turn * (nb - 1)
    cs = 1 + turn * (nb - 1)

    def at(fi, si):
        return fi * cf + si * cs

    def copy(src, dst, send, recv, where):
        return pltpu.make_async_remote_copy(
            src_ref=src, dst_ref=dst, send_sem=send, recv_sem=recv, device_id=where, device_id_type=MESH
        )

    loads = [
        pltpu.make_async_copy(source, target, ds.at[i])
        for i, (source, target) in enumerate(
            ((widths_ref, fills), (pattern_ref, fits), (anc_ref, anc_own), (panel_ref, panel_own))
        )
    ]
    for one in loads:
        one.start()

    first = (sec * ncol + col) * slots
    blocks = width // B

    def inside(j, i):
        return jnp.where(fills[first + j] > i, 1.0, 0.0).astype(F32)

    def present(j, r, c):
        return fits[first + j, r * blocks + c].astype(F32)

    def keep(src, j, h, slot, r):
        for i in range(h * wb // parts, (h + 1) * wb // parts):
            here = pl.ds(j * SW + i * B, B)
            for c in range(blocks):
                cols = pl.ds(c * B, B)
                high, low = split(src(i, cols) * (inside(j, i) * present(j, r, c)))
                ph[slot, here, cols] = high
                plo[slot, here, cols] = low

    has_left = (col > 0).astype(jnp.int32)
    has_right = (col < ncol - 1).astype(jnp.int32)
    barrier = pltpu.get_barrier_semaphore()
    for d in range(1, nrow):
        pl.semaphore_signal(barrier, inc=1, device_id={"row": (row + d) % nrow}, device_id_type=MESH)
    pl.semaphore_signal(barrier, inc=1, device_id={"sec": 1 - sec}, device_id_type=MESH)

    @pl.when(col > 0)
    def _():
        pl.semaphore_signal(barrier, inc=1, device_id={"col": col - 1}, device_id_type=MESH)

    @pl.when(col < ncol - 1)
    def _():
        pl.semaphore_signal(barrier, inc=1, device_id={"col": col + 1}, device_id_type=MESH)

    pl.semaphore_wait(barrier, nrow + has_left + has_right)

    mine = sec * ncol + col

    def piece_copy(src, p, way):
        where = ({"col": col - 1}, {"col": col + 1}, {"sec": 1 - sec})[way]
        size = src.shape[0] // CHUNKS
        return Group([
            copy(
                src.at[pl.ds(c * size, size)], anc.at[p, pl.ds(c * size, size)],
                zs.at[p, way, c], zr.at[p, c], where,
            )
            for c in range(CHUNKS)
        ])

    def opp_copy(src, d, e, k):
        return copy(
            src, opp.at[d - 1, e - 1, k], os_.at[d - 1, e - 1, k], or_.at[d - 1, e - 1, k],
            {"row": at((f + d) % nf, s)},
        )

    def pass_on(src, p):
        for d in range(1, nf):
            for e in range(1, ns):
                @pl.when(p // per == at((f + d) % nf, (s + e) % ns))
                def _():
                    opp_copy(src, d, e, p % per).start()

    def panel_copy(d, j, h):
        return copy(
            panel_ref.at[pl.ds(j * SW + h * tm, tm)], pin.at[d - 1, j, pl.ds(h * tm, tm)],
            ps.at[d - 1, j, h], pr.at[d - 1, j, h], {"row": at((f + d) % nf, s)},
        )

    def halves(src, p):
        high, low = split(src[...])
        ah[p] = high
        al[p] = low

    def late(p):
        return p // per == row

    def send_mine():
        pl.when(col > 0)(lambda: piece_copy(anc_ref, mine, 0).start())
        pl.when(col < ncol - 1)(lambda: piece_copy(anc_ref, mine, 1).start())
        piece_copy(anc_ref, mine, 2).start()

    other = (1 - sec) * ncol + col

    def panels_out():
        for j in range(slots):
            for h in range(parts):
                for d in range(1, nf):
                    panel_copy(d, j, h).start()

    def settle_own():
        for one in loads:
            one.wait()
        halves(anc_own, mine)
        for j in range(slots):
            for h in range(parts):
                keep(lambda i, cols: panel_own[pl.ds(j * SW + i * B, B), cols], j, h, 0, row)

    def relay(p, way, c, onward):
        piece_copy(anc_ref, p, way).copies[c].wait_recv()
        pl.when(onward)(lambda: piece_copy(anc.at[p], p, way).copies[c].start())
        piece_copy(anc.at[p], p, 2).copies[c].start()

    if crossed is not None:
        obuf, xs, xr, zos, zor = crossed
        half = width // 2
        osize = half // OCHUNKS

        def native(z):
            return (z // per != b).astype(jnp.int32)

        def early(side, z):
            return native(z) == (side == a).astype(jnp.int32)

        def cross_copies(axis):
            where = {"row": (1 - a) * nb + b} if axis == 0 else {"row": a * nb + 1 - b}
            k = col % per
            base = (k if axis == 0 else 1 - k) * half
            return Group([
                copy(
                    anc_ref.at[pl.ds(pl.multiple_of(base + c * osize, 8), osize)],
                    obuf.at[col, pl.ds(c * osize, osize)], xs.at[axis, c], xr.at[c], where,
                )
                for c in range(OCHUNKS)
            ])

        def o_copy(z, way):
            where = ({"col": col - 1}, {"col": col + 1}, {"sec": 1 - sec})[way]
            return Group([
                copy(
                    obuf.at[z, pl.ds(c * osize, osize)], obuf.at[z, pl.ds(c * osize, osize)],
                    zos.at[z, way, c], zor.at[z, c], where,
                )
                for c in range(OCHUNKS)
            ])

        is_early = early(sec, col)
        is_opp = jnp.logical_and(native(col) == 1, sec != a)

        @pl.when(is_opp)
        def _():
            cross_copies(0).start()
            cross_copies(1).start()

        at_end = jnp.logical_or(col == 0, col == ncol - 1)
        pl.when(is_early)(send_mine)
        panels_out()
        pl.when(jnp.logical_and(late(mine), at_end))(send_mine)
        settle_own()

        @pl.when(is_early)
        def _():
            for c in range(OCHUNKS):
                cross_copies(0).copies[c].wait_recv()
                pl.when(col > 0)(lambda: o_copy(col, 0).copies[c].start())
                pl.when(col < ncol - 1)(lambda: o_copy(col, 1).copies[c].start())
                o_copy(col, 2).copies[c].start()

        def o_relay(z, way, c, onward):
            o_copy(z, way).copies[c].wait_recv()
            pl.when(onward)(lambda: o_copy(z, way).copies[c].start())
            o_copy(z, 2).copies[c].start()

        def from_partner(z):
            p = (1 - sec) * ncol + z
            piece_copy(anc_ref, p, 2).wait_recv()
            o_copy(z, 2).wait_recv()
            halves(anc.at[p], p)

        def early_step(t, carry):
            left = jnp.logical_and(col - t >= 0, early(sec, col - t))
            right = jnp.logical_and(col + t < ncol, early(sec, col + t))
            for c in range(CHUNKS):
                pl.when(left)(lambda: relay(mine - t, 1, c, col < ncol - 1))
                pl.when(right)(lambda: relay(mine + t, 0, c, col > 0))
            for c in range(OCHUNKS):
                pl.when(left)(lambda: o_relay(col - t, 1, c, col < ncol - 1))
                pl.when(right)(lambda: o_relay(col + t, 0, c, col > 0))
            pl.when(left)(lambda: halves(anc.at[mine - t], mine - t))
            pl.when(right)(lambda: halves(anc.at[mine + t], mine + t))
            left = jnp.logical_and(col - t >= 0, early(1 - sec, col - t))
            right = jnp.logical_and(col + t < ncol, early(1 - sec, col + t))
            pl.when(left)(lambda: from_partner(col - t))
            pl.when(right)(lambda: from_partner(col + t))
            return carry

        def spot(z):
            k = z % per
            return jnp.where(jnp.logical_or(native(z) == 1, sec == 1), k, 1 - k)

        def place(z):
            k = z % per
            seen = native(z)
            turned = seen == sec
            rpos = jnp.where(jnp.logical_or(seen == 1, sec == 0), k, 1 - k)
            here = pl.ds(pl.multiple_of(rpos * half, half), half)

            def put(value):
                high, low = split(value)
                oh[0, 0, spot(z), here] = high
                ol[0, 0, spot(z), here] = low

            pl.when(turned)(lambda: put(obuf[z].T))
            pl.when(jnp.logical_not(turned))(lambda: put(obuf[z]))

        def late_partner(p):
            piece_copy(anc_ref, p, 2).wait_recv()
            halves(anc.at[p], p)

        def late_step(t, ends, here):
            def wanted(p, z):
                edge = jnp.logical_or(z == 0, z == ncol - 1)
                return jnp.logical_and(jnp.logical_and(late(p), here), edge if ends else jnp.logical_not(edge))

            left = jnp.logical_and(col - t >= 0, wanted(mine - t, col - t))
            right = jnp.logical_and(col + t < ncol, wanted(mine + t, col + t))
            for c in range(CHUNKS):
                pl.when(left)(lambda: relay(mine - t, 1, c, col < ncol - 1))
                pl.when(right)(lambda: relay(mine + t, 0, c, col > 0))
            pl.when(left)(lambda: halves(anc.at[mine - t], mine - t))
            pl.when(right)(lambda: halves(anc.at[mine + t], mine + t))

        def late_partners(t):
            left = jnp.logical_and(col - t >= 0, late(other - t))
            right = jnp.logical_and(col + t < ncol, late(other + t))
            pl.when(left)(lambda: late_partner(other - t))
            pl.when(right)(lambda: late_partner(other + t))

    else:
        @pl.when(jnp.logical_not(late(mine)))
        def _():
            send_mine()
            pass_on(anc_ref, mine)

        panels_out()
        settle_own()

        def settle(p):
            pass_on(anc.at[p], p)
            halves(anc.at[p], p)

        def from_partner(p):
            piece_copy(anc_ref, p, 2).wait_recv()
            pass_on(anc.at[p], p)
            halves(anc.at[p], p)

        def gather(phase):
            def ready(p):
                return late(p) if phase else jnp.logical_not(late(p))

            def step(t, carry):
                left = jnp.logical_and(col - t >= 0, ready(mine - t))
                right = jnp.logical_and(col + t < ncol, ready(mine + t))
                for c in range(CHUNKS):
                    pl.when(left)(lambda: relay(mine - t, 1, c, col < ncol - 1))
                    pl.when(right)(lambda: relay(mine + t, 0, c, col > 0))
                pl.when(left)(lambda: settle(mine - t))
                pl.when(right)(lambda: settle(mine + t))
                partners(t)
                return carry

            def partners(t):
                left = jnp.logical_and(col - t >= 0, ready(other - t))
                right = jnp.logical_and(col + t < ncol, ready(other + t))
                pl.when(left)(lambda: from_partner(other - t))
                pl.when(jnp.logical_and(right, t > 0))(lambda: from_partner(other + t))

            partners(0)
            lax.fori_loop(1, ncol, step, 0)

        gather(0)
        pl.when(late(mine))(send_mine)
        for d in range(1, nf):
            for e in range(1, ns):
                for k in range(per):
                    opp_copy(anc_ref, d, e, k).wait_recv()
                    high, low = split(opp[d - 1, e - 1, k])
                    oh[d - 1, e - 1, k] = high
                    ol[d - 1, e - 1, k] = low

    def q_copy(e, k, j, h):
        rr = pl.ds(j * SW + h * tm, tm)
        return copy(
            qsend.at[e - 1, k, rr], qrecv.at[e - 1, k, rr], qs.at[e - 1, k, j, h], qr.at[e - 1, k, j, h],
            {"row": at(f, (s + e) % ns)},
        )

    def products(k, fresh, pause=None):
        for j in range(slots):
            for h in range(parts):
                rr = pl.ds(j * SW + h * tm, tm)
                if pause is not None and (j + 1) * (h + 1) == slots * parts:
                    pause()
                for d in range(1, nf):
                    if fresh:
                        panel_copy(d, j, h).wait_recv()
                        keep(lambda i, cols: pin[d - 1, j, pl.ds(i * B, B), cols], j, h, d, at((f + nf - d) % nf, s))
                for e in range(1, ns):
                    p = at(f, (s + e) % ns) * per + k
                    acc = dot3(ph[0, rr], plo[0, rr], ah[p], al[p], NN)
                    for d in range(1, nf):
                        acc += dot3(ph[d, rr], plo[d, rr], oh[d - 1, e - 1, k], ol[d - 1, e - 1, k], NN)
                    qsend[e - 1, k, rr] = acc
                    q_copy(e, k, j, h).start()

    if crossed is not None:
        last = ncol - 1 - col
        pl.when(early(1 - sec, col))(lambda: from_partner(col))
        lax.fori_loop(1, ncol - 1, early_step, 0)
        pl.when(jnp.logical_and(late(mine), jnp.logical_not(at_end)))(send_mine)
        middle = jnp.logical_not(at_end)

        def forward_late():
            late_step(1, False, middle)
            late_step(2, True, middle)

        late_step(1, True, middle)
        for z in range(ncol):
            pl.when(z != last)(functools.partial(place, z))
        products(1 - spot(last), True, forward_late)
        early_step(ncol - 1, 0)
        place(last)
        products(spot(last), False)
    else:
        for k in range(per):
            products(k, k == 0)

    def near(i, carry):
        rr = pl.ds(pl.multiple_of(i * tm, tm), tm)
        acc = jnp.zeros((tm, width), F32)
        for d in range(1, nf):
            for k in range(per):
                p = at((f + nf - d) % nf, s) * per + k
                cols = pl.ds(k * pw, pw)
                acc += dot3(ph[d, rr, cols], plo[d, rr, cols], ah[p], al[p], NT)
        prod_ref[rr] = acc
        return carry

    lax.fori_loop(0, rows // tm, near, 0)
    if crossed is not None:
        pl.when(late(other))(lambda: late_partner(other))
        late_step(1, False, at_end)
        late_partners(1)
        late_step(2, False, at_end)
        late_partners(2)
        late_step(ncol - 1, True, at_end)
        late_partners(ncol - 1)
    else:
        gather(1)

    def own(i, carry):
        rr = pl.ds(pl.multiple_of(i * tm, tm), tm)
        for k in range(per):
            p = row * per + k
            prod_ref[rr, pl.ds(k * pw, pw)] += dot3(ph[0, rr], plo[0, rr], ah[p], al[p], NN)
        return carry

    lax.fori_loop(0, rows // tm, own, 0)

    span = nf * part

    def portion(i):
        return pl.ds(pl.multiple_of(i * span, 8), span)

    def across(d):
        return {"row": at(f, (s + d) % ns)}

    def along(d):
        return {"row": at((f + d) % nf, s)}

    def u_copy(j, d):
        return copy(
            upack.at[j, portion((s + d) % ns)], urecv.at[j, d - 1], us.at[j, d - 1], ur.at[j, d - 1], across(d)
        )

    def v_copy(j, d):
        return copy(
            usum.at[j, pl.ds(pl.multiple_of(((f + d) % nf) * part, 8), part)],
            urecv2.at[j, d - 1], us2.at[j, d - 1], ur2.at[j, d - 1], along(d),
        )

    def h_copy(j, d):
        done = pl.ds(pl.multiple_of((s * nf + f) * part, 8), part)
        return copy(ufin.at[j, done], ufin.at[j, done], gs2.at[j, d - 1], gr2.at[j, d - 1], along(d))

    def g_copy(j, d):
        return copy(ufin.at[j, portion(s)], ufin.at[j, portion(s)], gs.at[j, d - 1], gr.at[j, d - 1], across(d))

    ri = lax.broadcasted_iota(jnp.int32, (B, B), 0)
    ci = lax.broadcasted_iota(jnp.int32, (B, B), 1)
    rows8 = lax.broadcasted_iota(jnp.int32, (8, B), 0)
    offs, tail = spots(wb)

    def update_out(j):
        for h in range(parts):
            rr = pl.ds(j * SW + h * tm, tm)
            for e in range(1, ns):
                for k in range(per):
                    q_copy(e, k, j, h).wait_recv()
                    prod_ref[rr, pl.ds(k * pw, pw)] += qrecv[e - 1, k, rr]
        extra = jnp.zeros((8, B), F32)
        held = None
        for i in range(wb):
            qh, ql = split(prod_ref[pl.ds(j * SW + i * B, B)])
            rest = pl.ds(j * SW + i * B, SW - i * B)
            line = dot3(qh, ql, ph[0, rest], plo[0, rest], NT)
            for k in range(i + 1, wb):
                upack[j, pl.ds(offs[i, k], B)] = line[:, (k - i) * B:(k - i + 1) * B]
            if i % 2 == 0:
                held = line[:, :B]
            else:
                low = line[:, :B]
                upack[j, pl.ds(i // 2 * B, B)] = jnp.where(ri <= ci, held, low)
                mid = jnp.sum(jnp.where(ri == ci, low, 0.0), axis=0, keepdims=True)
                extra = jnp.where(rows8 == i // 2, mid, extra)
        upack[j, pl.ds(tail, 8)] = extra
        upack[j, pl.ds(tail + 8, 8 * (nrow - 1))] = jnp.zeros((8 * (nrow - 1), B), F32)
        for d in range(1, ns):
            u_copy(j, d).start()

    def negate(j):
        for i in range(wb):
            here = pl.ds(j * SW + i * B, B)
            for c in range(blocks):
                cols = pl.ds(c * B, B)
                prod_ref[here, cols] = prod_ref[here, cols] * -(inside(j, i) * present(j, row, c))

    def second(j):
        negate(j)
        for d in range(1, ns):
            u_copy(j, d).wait_recv()
        total = upack[j, portion(s)]
        for d in range(1, ns):
            total += urecv[j, d - 1]
        usum[j] = total
        for d in range(1, nf):
            v_copy(j, d).start()

    def third(j):
        for d in range(1, nf):
            v_copy(j, d).wait_recv()
        total = usum[j, pl.ds(pl.multiple_of(f * part, 8), part)]
        for d in range(1, nf):
            total += urecv2[j, d - 1]
        ufin[j, pl.ds(pl.multiple_of((s * nf + f) * part, 8), part)] = total
        for d in range(1, nf):
            h_copy(j, d).start()

    def fourth(j):
        for d in range(1, nf):
            h_copy(j, d).wait_recv()
        for d in range(1, ns):
            g_copy(j, d).start()

    def finish(j):
        for d in range(1, ns):
            g_copy(j, d).wait_recv()
        sum_ref[j] = ufin[j]
        for i in range(wb):
            sum_ref[j, pl.ds(tail + 8 + i, 1)] = jnp.broadcast_to(inside(j, i), (1, B))

    stages = [update_out, second, third, fourth]
    for step in range(slots - 1 + len(stages)):
        for j in reversed(range(slots)):
            if 0 <= step - j < len(stages):
                stages[step - j](j)
    for j in range(slots):
        finish(j)

    for j in range(slots):
        for d in range(1, ns):
            u_copy(j, d).wait_send()
            g_copy(j, d).wait_send()
        for d in range(1, nf):
            v_copy(j, d).wait_send()
            h_copy(j, d).wait_send()
        for h in range(parts):
            for e in range(1, ns):
                for k in range(per):
                    q_copy(e, k, j, h).wait_send()
            for d in range(1, nf):
                panel_copy(d, j, h).wait_send()

    if crossed is None:
        for d in range(1, nf):
            for e in range(1, ns):
                for k in range(per):
                    opp_copy(anc_ref, d, e, k).wait_send()

    def drain(q, carry):
        p = sec * ncol + q
        to_right = jnp.logical_and(q <= col, col < ncol - 1)
        to_left = jnp.logical_and(q >= col, col > 0)
        if crossed is None:
            sent = q >= 0
        else:
            sent = jnp.logical_or(early(sec, q), late(p))
        pl.when(jnp.logical_and(sent, to_right))(lambda: piece_copy(anc_ref, p, 1).wait_send())
        pl.when(jnp.logical_and(sent, to_left))(lambda: piece_copy(anc_ref, p, 0).wait_send())
        pl.when(sent)(lambda: piece_copy(anc_ref, p, 2).wait_send())
        if crossed is not None:
            first_half = early(sec, q)
            pl.when(jnp.logical_and(first_half, to_right))(lambda: o_copy(q, 1).wait_send())
            pl.when(jnp.logical_and(first_half, to_left))(lambda: o_copy(q, 0).wait_send())
            pl.when(first_half)(lambda: o_copy(q, 2).wait_send())
        return carry

    lax.fori_loop(0, ncol, drain, 0)
    if crossed is not None:
        @pl.when(is_opp)
        def _():
            cross_copies(0).wait_send()
            cross_copies(1).wait_send()


def write_out(parts, prod_ref, sum_ref, diag_ref, off_ref, upd_ref):
    h = pl.program_id(1)
    wb = SW // B
    each = wb // parts
    offs, tail = spots(wb)
    ri = lax.broadcasted_iota(jnp.int32, (B, B), 0)
    ci = lax.broadcasted_iota(jnp.int32, (B, B), 1)
    off_ref[...] = prod_ref[...]

    def inside(i):
        return sum_ref[0, pl.ds(tail + 8 + i, 1)]

    def block_of(i, k):
        if i < k:
            return sum_ref[0, pl.ds(offs[i, k], B)]
        if i > k:
            return sum_ref[0, pl.ds(offs[k, i], B)].T
        both = sum_ref[0, pl.ds(i // 2 * B, B)]
        if i % 2 == 0:
            return jnp.where(ri <= ci, both, both.T)
        return jnp.where(ri == ci, sum_ref[0, pl.ds(tail + i // 2, 1)], jnp.where(ri > ci, both, both.T))

    for part in range(parts):
        @pl.when(h == part)
        def _():
            for i in range(each):
                for k in range(wb):
                    here = (pl.ds(i * B, B), pl.ds(k * B, B))
                    upd_ref[here] = (diag_ref[here] + block_of(part * each + i, k)) * inside(max(part * each + i, k))


def local(sizes, anc_inverse, panel, diag_inverse, widths, pattern):
    nsec, nrow, ncol, nf, ns, nb, square = sizes
    rows, width = panel.shape
    pw = anc_inverse.shape[1]
    per = width // pw
    slots = rows // SW
    pieces = nsec * ncol
    packed = packed_rows(nrow)
    part = packed // nrow
    parts = SW // TM
    short = square and nsec == nb == per == 2 and ncol == per * nb
    vm = pltpu.VMEM
    dma = pltpu.SemaphoreType.DMA
    whole = pl.BlockSpec(memory_space=pltpu.VMEM)
    far = pl.BlockSpec(memory_space=pltpu.HBM)
    product, summed = pl.pallas_call(
        functools.partial(kernel, sizes),
        out_shape=(jax.ShapeDtypeStruct((rows, width), F32), jax.ShapeDtypeStruct((slots, packed, B), F32)),
        in_specs=[far, far, far, far],
        out_specs=(whole, whole),
        scratch_shapes=[
            vm((pieces, width, pw), F32),
            vm((pieces, width, pw), BF),
            vm((pieces, width, pw), BF),
            vm((nf, rows, width), BF),
            vm((nf, rows, width), BF),
            vm((nf - 1, slots, SW, width), F32),
            None if short else vm((nf - 1, ns - 1, per, width, pw), F32),
            vm((nf - 1, ns - 1, per, width, pw), BF),
            vm((nf - 1, ns - 1, per, width, pw), BF),
            vm((ns - 1, per, rows, pw), F32),
            vm((ns - 1, per, rows, pw), F32),
            vm((slots, packed, B), F32),
            vm((slots, ns - 1, nf * part, B), F32),
            vm((slots, nf * part, B), F32),
            vm((slots, nf - 1, part, B), F32),
            vm((slots, packed, B), F32),
            dma((pieces, 3, CHUNKS)), dma((pieces, CHUNKS)),
            dma((nf - 1, slots, parts)), dma((nf - 1, slots, parts)),
            None if short else dma((nf - 1, ns - 1, per)), None if short else dma((nf - 1, ns - 1, per)),
            dma((ns - 1, per, slots, parts)), dma((ns - 1, per, slots, parts)),
            dma((slots, ns - 1)), dma((slots, ns - 1)),
            dma((slots, nf - 1)), dma((slots, nf - 1)),
            dma((slots, nf - 1)), dma((slots, nf - 1)),
            dma((slots, ns - 1)), dma((slots, ns - 1)),
            vm((width, pw), F32), vm((rows, width), F32),
            pltpu.SMEM(widths.shape, widths.dtype), pltpu.SMEM(pattern.shape, pattern.dtype), dma((4,)),
            (
                vm((ncol, width // 2, pw), F32), dma((2, OCHUNKS)), dma((OCHUNKS,)),
                dma((ncol, 3, OCHUNKS)), dma((ncol, OCHUNKS)),
            ) if short else None,
        ],
        compiler_params=pltpu.CompilerParams(
            collective_id=0, has_side_effects=True, vmem_limit_bytes=(49 if short else 60) * 1024 * 1024
        ),
    )(anc_inverse, panel, widths, pattern)
    strip = pl.BlockSpec((TM, width), lambda j, h: (j * parts + h, 0))
    square_strip = pl.BlockSpec((TM, SW), lambda j, h: (j * parts + h, 0))
    return pl.pallas_call(
        functools.partial(write_out, parts),
        grid=(slots, parts),
        out_shape=(jax.ShapeDtypeStruct((rows, width), F32), jax.ShapeDtypeStruct((rows, SW), F32)),
        in_specs=[strip, pl.BlockSpec((1, packed, B), lambda j, h: (j, 0, 0)), square_strip],
        out_specs=(strip, square_strip),
        compiler_params=pltpu.CompilerParams(vmem_limit_bytes=16 * 1024 * 1024),
    )(product, summed, diag_inverse)


def solution(mesh):
    shape = dict(mesh.shape)
    na, nb = factor(shape["row"])
    sizes = (shape["sec"], shape["row"], shape["col"], na, nb, nb, na == nb)
    in_specs = (
        P("row", ("sec", "col")),
        P(("sec", "col"), "row"),
        P(("sec", "col"), None),
        P(),
        P(),
    )
    out_specs = (P(("sec", "col"), "row"), P(("sec", "col"), None))
    return jax.shard_map(
        functools.partial(local, sizes), mesh=mesh, in_specs=in_specs, out_specs=out_specs, check_vma=False
    )
```

```python
import functools
import jax
import jax.numpy as jnp
from jax import lax
from jax.experimental import pallas as pl
from jax.experimental.pallas import tpu as pltpu
from jax.sharding import PartitionSpec as P

B = 128
SW = 512
CHUNKS = 8
OCHUNKS = 4
TM = 256
F32 = jnp.float32
BF = jnp.bfloat16
MESH = pl.DeviceIdType.MESH
NN = (((1,), (0,)), ((), ()))
NT = (((1,), (1,)), ((), ()))


def split(value):
    high = value.astype(BF)
    return high, (value - high.astype(F32)).astype(BF)


def dot3(ah, al, bh, bl, dims):
    dot = functools.partial(lax.dot_general, dimension_numbers=dims, preferred_element_type=F32)
    return dot(ah, bh) + (dot(ah, bl) + dot(al, bh))


def packed_rows(nrow):
    wb = SW // B
    return (wb * (wb + 1) // 2 - wb // 2) * B + 8 * nrow


def spots(wb):
    offs = {}
    for i in range(wb):
        for k in range(i + 1, wb):
            offs[i, k] = (wb // 2 + len(offs)) * B
    return offs, (wb // 2 + len(offs)) * B


def factor(count):
    low = 1
    for value in range(1, count + 1):
        if count % value == 0 and value * value <= count:
            low = value
    return count // low, low


class Group:
    def __init__(self, copies):
        self.copies = copies

    def start(self):
        for one in self.copies:
            one.start()

    def wait_recv(self):
        for one in self.copies:
            one.wait_recv()

    def wait_send(self):
        for one in self.copies:
            one.wait_send()


def kernel(
    sizes,
    anc_ref, panel_ref, widths_ref, pattern_ref, prod_ref, sum_ref,
    anc, ah, al, ph, plo, pin, opp, oh, ol, qsend, qrecv, upack, urecv, usum, urecv2, ufin,
    zs, zr, ps, pr, os_, or_, qs, qr, us, ur, us2, ur2, gs2, gr2, gs, gr, anc_own, panel_own, fills, fits, ds, crossed,
):
    nsec, nrow, ncol, nf, ns, nb, square = sizes
    rows, width = panel_ref.shape
    pw = anc_ref.shape[1]
    per = width // pw
    slots = rows // SW
    wb = SW // B
    part = packed_rows(nrow) // nrow
    tm = TM
    parts = SW // tm
    sec, row, col = lax.axis_index("sec"), lax.axis_index("row"), lax.axis_index("col")
    turn = sec if square else 0
    a, b = row // nb, row % nb
    f = a + turn * (b - a)
    s = b + turn * (a - b)
    cf = nb - turn * (nb - 1)
    cs = 1 + turn * (nb - 1)

    def at(fi, si):
        return fi * cf + si * cs

    def copy(src, dst, send, recv, where):
        return pltpu.make_async_remote_copy(
            src_ref=src, dst_ref=dst, send_sem=send, recv_sem=recv, device_id=where, device_id_type=MESH
        )

    loads = [
        pltpu.make_async_copy(source, target, ds.at[i])
        for i, (source, target) in enumerate(
            ((widths_ref, fills), (pattern_ref, fits), (anc_ref, anc_own), (panel_ref, panel_own))
        )
    ]
    for one in loads:
        one.start()

    first = (sec * ncol + col) * slots
    blocks = width // B

    def inside(j, i):
        return jnp.where(fills[first + j] > i, 1.0, 0.0).astype(F32)

    def present(j, r, c):
        return fits[first + j, r * blocks + c].astype(F32)

    def keep(src, j, h, slot, r):
        for i in range(h * wb // parts, (h + 1) * wb // parts):
            here = pl.ds(j * SW + i * B, B)
            for c in range(blocks):
                cols = pl.ds(c * B, B)
                high, low = split(src(i, cols) * (inside(j, i) * present(j, r, c)))
                ph[slot, here, cols] = high
                plo[slot, here, cols] = low

    has_left = (col > 0).astype(jnp.int32)
    has_right = (col < ncol - 1).astype(jnp.int32)
    barrier = pltpu.get_barrier_semaphore()
    for d in range(1, nrow):
        pl.semaphore_signal(barrier, inc=1, device_id={"row": (row + d) % nrow}, device_id_type=MESH)
    pl.semaphore_signal(barrier, inc=1, device_id={"sec": 1 - sec}, device_id_type=MESH)

    @pl.when(col > 0)
    def _():
        pl.semaphore_signal(barrier, inc=1, device_id={"col": col - 1}, device_id_type=MESH)

    @pl.when(col < ncol - 1)
    def _():
        pl.semaphore_signal(barrier, inc=1, device_id={"col": col + 1}, device_id_type=MESH)

    pl.semaphore_wait(barrier, nrow + has_left + has_right)

    mine = sec * ncol + col

    def piece_copy(src, p, way):
        where = ({"col": col - 1}, {"col": col + 1}, {"sec": 1 - sec})[way]
        size = src.shape[0] // CHUNKS
        return Group([
            copy(
                src.at[pl.ds(c * size, size)], anc.at[p, pl.ds(c * size, size)],
                zs.at[p, way, c], zr.at[p, c], where,
            )
            for c in range(CHUNKS)
        ])

    def opp_copy(src, d, e, k):
        return copy(
            src, opp.at[d - 1, e - 1, k], os_.at[d - 1, e - 1, k], or_.at[d - 1, e - 1, k],
            {"row": at((f + d) % nf, s)},
        )

    def pass_on(src, p):
        for d in range(1, nf):
            for e in range(1, ns):
                @pl.when(p // per == at((f + d) % nf, (s + e) % ns))
                def _():
                    opp_copy(src, d, e, p % per).start()

    def panel_copy(d, j, h):
        return copy(
            panel_ref.at[pl.ds(j * SW + h * tm, tm)], pin.at[d - 1, j, pl.ds(h * tm, tm)],
            ps.at[d - 1, j, h], pr.at[d - 1, j, h], {"row": at((f + d) % nf, s)},
        )

    def halves(src, p):
        high, low = split(src[...])
        ah[p] = high
        al[p] = low

    def late(p):
        return p // per == row

    def send_mine():
        pl.when(col > 0)(lambda: piece_copy(anc_ref, mine, 0).start())
        pl.when(col < ncol - 1)(lambda: piece_copy(anc_ref, mine, 1).start())
        piece_copy(anc_ref, mine, 2).start()

    other = (1 - sec) * ncol + col

    def panels_out():
        for j in range(slots):
            for h in range(parts):
                for d in range(1, nf):
                    panel_copy(d, j, h).start()

    def settle_own():
        for one in loads:
            one.wait()
        halves(anc_own, mine)
        for j in range(slots):
            for h in range(parts):
                keep(lambda i, cols: panel_own[pl.ds(j * SW + i * B, B), cols], j, h, 0, row)

    def relay(p, way, c, onward):
        piece_copy(anc_ref, p, way).copies[c].wait_recv()
        pl.when(onward)(lambda: piece_copy(anc.at[p], p, way).copies[c].start())
        piece_copy(anc.at[p], p, 2).copies[c].start()

    if crossed is not None:
        obuf, xs, xr, zos, zor = crossed
        half = width // 2
        osize = half // OCHUNKS

        def native(z):
            return (z // per != b).astype(jnp.int32)

        def early(side, z):
            return native(z) == (side == a).astype(jnp.int32)

        def cross_copies(axis):
            where = {"row": (1 - a) * nb + b} if axis == 0 else {"row": a * nb + 1 - b}
            k = col % per
            base = (k if axis == 0 else 1 - k) * half
            return Group([
                copy(
                    anc_ref.at[pl.ds(pl.multiple_of(base + c * osize, 8), osize)],
                    obuf.at[col, pl.ds(c * osize, osize)], xs.at[axis, c], xr.at[c], where,
                )
                for c in range(OCHUNKS)
            ])

        def o_copy(z, way):
            where = ({"col": col - 1}, {"col": col + 1}, {"sec": 1 - sec})[way]
            return Group([
                copy(
                    obuf.at[z, pl.ds(c * osize, osize)], obuf.at[z, pl.ds(c * osize, osize)],
                    zos.at[z, way, c], zor.at[z, c], where,
                )
                for c in range(OCHUNKS)
            ])

        is_early = early(sec, col)
        is_opp = jnp.logical_and(native(col) == 1, sec != a)

        @pl.when(is_opp)
        def _():
            cross_copies(0).start()
            cross_copies(1).start()

        at_end = jnp.logical_or(col == 0, col == ncol - 1)
        pl.when(is_early)(send_mine)
        panels_out()
        pl.when(jnp.logical_and(late(mine), at_end))(send_mine)
        settle_own()

        @pl.when(is_early)
        def _():
            for c in range(OCHUNKS):
                cross_copies(0).copies[c].wait_recv()
                pl.when(col > 0)(lambda: o_copy(col, 0).copies[c].start())
                pl.when(col < ncol - 1)(lambda: o_copy(col, 1).copies[c].start())
                o_copy(col, 2).copies[c].start()

        def o_relay(z, way, c, onward):
            o_copy(z, way).copies[c].wait_recv()
            pl.when(onward)(lambda: o_copy(z, way).copies[c].start())
            o_copy(z, 2).copies[c].start()

        def from_partner(z):
            p = (1 - sec) * ncol + z
            piece_copy(anc_ref, p, 2).wait_recv()
            o_copy(z, 2).wait_recv()
            halves(anc.at[p], p)

        def early_step(t, carry):
            left = jnp.logical_and(col - t >= 0, early(sec, col - t))
            right = jnp.logical_and(col + t < ncol, early(sec, col + t))
            for c in range(CHUNKS):
                pl.when(left)(lambda: relay(mine - t, 1, c, col < ncol - 1))
                pl.when(right)(lambda: relay(mine + t, 0, c, col > 0))
            for c in range(OCHUNKS):
                pl.when(left)(lambda: o_relay(col - t, 1, c, col < ncol - 1))
                pl.when(right)(lambda: o_relay(col + t, 0, c, col > 0))
            pl.when(left)(lambda: halves(anc.at[mine - t], mine - t))
            pl.when(right)(lambda: halves(anc.at[mine + t], mine + t))
            left = jnp.logical_and(col - t >= 0, early(1 - sec, col - t))
            right = jnp.logical_and(col + t < ncol, early(1 - sec, col + t))
            pl.when(left)(lambda: from_partner(col - t))
            pl.when(right)(lambda: from_partner(col + t))
            return carry

        def spot(z):
            k = z % per
            return jnp.where(jnp.logical_or(native(z) == 1, sec == 1), k, 1 - k)

        def place(z):
            k = z % per
            seen = native(z)
            turned = seen == sec
            rpos = jnp.where(jnp.logical_or(seen == 1, sec == 0), k, 1 - k)
            here = pl.ds(pl.multiple_of(rpos * half, half), half)

            def put(value):
                high, low = split(value)
                oh[0, 0, spot(z), here] = high
                ol[0, 0, spot(z), here] = low

            pl.when(turned)(lambda: put(obuf[z].T))
            pl.when(jnp.logical_not(turned))(lambda: put(obuf[z]))

        def late_partner(p):
            piece_copy(anc_ref, p, 2).wait_recv()
            halves(anc.at[p], p)

        def late_step(t, ends, here):
            def wanted(p, z):
                edge = jnp.logical_or(z == 0, z == ncol - 1)
                return jnp.logical_and(jnp.logical_and(late(p), here), edge if ends else jnp.logical_not(edge))

            left = jnp.logical_and(col - t >= 0, wanted(mine - t, col - t))
            right = jnp.logical_and(col + t < ncol, wanted(mine + t, col + t))
            for c in range(CHUNKS):
                pl.when(left)(lambda: relay(mine - t, 1, c, col < ncol - 1))
                pl.when(right)(lambda: relay(mine + t, 0, c, col > 0))
            pl.when(left)(lambda: halves(anc.at[mine - t], mine - t))
            pl.when(right)(lambda: halves(anc.at[mine + t], mine + t))

        def late_partners(t):
            left = jnp.logical_and(col - t >= 0, late(other - t))
            right = jnp.logical_and(col + t < ncol, late(other + t))
            pl.when(left)(lambda: late_partner(other - t))
            pl.when(right)(lambda: late_partner(other + t))

    else:
        @pl.when(jnp.logical_not(late(mine)))
        def _():
            send_mine()
            pass_on(anc_ref, mine)

        panels_out()
        settle_own()

        def settle(p):
            pass_on(anc.at[p], p)
            halves(anc.at[p], p)

        def from_partner(p):
            piece_copy(anc_ref, p, 2).wait_recv()
            pass_on(anc.at[p], p)
            halves(anc.at[p], p)

        def gather(phase):
            def ready(p):
                return late(p) if phase else jnp.logical_not(late(p))

            def step(t, carry):
                left = jnp.logical_and(col - t >= 0, ready(mine - t))
                right = jnp.logical_and(col + t < ncol, ready(mine + t))
                for c in range(CHUNKS):
                    pl.when(left)(lambda: relay(mine - t, 1, c, col < ncol - 1))
                    pl.when(right)(lambda: relay(mine + t, 0, c, col > 0))
                pl.when(left)(lambda: settle(mine - t))
                pl.when(right)(lambda: settle(mine + t))
                partners(t)
                return carry

            def partners(t):
                left = jnp.logical_and(col - t >= 0, ready(other - t))
                right = jnp.logical_and(col + t < ncol, ready(other + t))
                pl.when(left)(lambda: from_partner(other - t))
                pl.when(jnp.logical_and(right, t > 0))(lambda: from_partner(other + t))

            partners(0)
            lax.fori_loop(1, ncol, step, 0)

        gather(0)
        pl.when(late(mine))(send_mine)
        for d in range(1, nf):
            for e in range(1, ns):
                for k in range(per):
                    opp_copy(anc_ref, d, e, k).wait_recv()
                    high, low = split(opp[d - 1, e - 1, k])
                    oh[d - 1, e - 1, k] = high
                    ol[d - 1, e - 1, k] = low

    def q_copy(e, k, j, h):
        rr = pl.ds(j * SW + h * tm, tm)
        return copy(
            qsend.at[e - 1, k, rr], qrecv.at[e - 1, k, rr], qs.at[e - 1, k, j, h], qr.at[e - 1, k, j, h],
            {"row": at(f, (s + e) % ns)},
        )

    def products(k, fresh, pause=None):
        for j in range(slots):
            for h in range(parts):
                rr = pl.ds(j * SW + h * tm, tm)
                if pause is not None and (j + 1) * (h + 1) == slots * parts:
                    pause()
                for d in range(1, nf):
                    if fresh:
                        panel_copy(d, j, h).wait_recv()
                        keep(lambda i, cols: pin[d - 1, j, pl.ds(i * B, B), cols], j, h, d, at((f + nf - d) % nf, s))
                for e in range(1, ns):
                    p = at(f, (s + e) % ns) * per + k
                    acc = dot3(ph[0, rr], plo[0, rr], ah[p], al[p], NN)
                    for d in range(1, nf):
                        acc += dot3(ph[d, rr], plo[d, rr], oh[d - 1, e - 1, k], ol[d - 1, e - 1, k], NN)
                    qsend[e - 1, k, rr] = acc
                    q_copy(e, k, j, h).start()

    if crossed is not None:
        last = ncol - 1 - col
        pl.when(early(1 - sec, col))(lambda: from_partner(col))
        lax.fori_loop(1, ncol - 1, early_step, 0)
        pl.when(jnp.logical_and(late(mine), jnp.logical_not(at_end)))(send_mine)
        middle = jnp.logical_not(at_end)

        def forward_late():
            late_step(1, False, middle)
            late_step(2, True, middle)

        late_step(1, True, middle)
        for z in range(ncol):
            pl.when(z != last)(functools.partial(place, z))
        products(1 - spot(last), True, forward_late)
        early_step(ncol - 1, 0)
        place(last)
        products(spot(last), False)
    else:
        for k in range(per):
            products(k, k == 0)

    def near(i, carry):
        rr = pl.ds(pl.multiple_of(i * tm, tm), tm)
        acc = jnp.zeros((tm, width), F32)
        for d in range(1, nf):
            for k in range(per):
                p = at((f + nf - d) % nf, s) * per + k
                cols = pl.ds(k * pw, pw)
                acc += dot3(ph[d, rr, cols], plo[d, rr, cols], ah[p], al[p], NT)
        prod_ref[rr] = acc
        return carry

    lax.fori_loop(0, rows // tm, near, 0)
    if crossed is not None:
        pl.when(late(other))(lambda: late_partner(other))
        late_step(1, False, at_end)
        late_partners(1)
        late_step(2, False, at_end)
        late_partners(2)
        late_step(ncol - 1, True, at_end)
        late_partners(ncol - 1)
    else:
        gather(1)

    def own(i, carry):
        rr = pl.ds(pl.multiple_of(i * tm, tm), tm)
        for k in range(per):
            p = row * per + k
            prod_ref[rr, pl.ds(k * pw, pw)] += dot3(ph[0, rr], plo[0, rr], ah[p], al[p], NN)
        return carry

    lax.fori_loop(0, rows // tm, own, 0)

    span = nf * part

    def portion(i):
        return pl.ds(pl.multiple_of(i * span, 8), span)

    def across(d):
        return {"row": at(f, (s + d) % ns)}

    def along(d):
        return {"row": at((f + d) % nf, s)}

    def u_copy(j, d):
        return copy(
            upack.at[j, portion((s + d) % ns)], urecv.at[j, d - 1], us.at[j, d - 1], ur.at[j, d - 1], across(d)
        )

    def v_copy(j, d):
        return copy(
            usum.at[j, pl.ds(pl.multiple_of(((f + d) % nf) * part, 8), part)],
            urecv2.at[j, d - 1], us2.at[j, d - 1], ur2.at[j, d - 1], along(d),
        )

    def h_copy(j, d):
        done = pl.ds(pl.multiple_of((s * nf + f) * part, 8), part)
        return copy(ufin.at[j, done], ufin.at[j, done], gs2.at[j, d - 1], gr2.at[j, d - 1], along(d))

    def g_copy(j, d):
        return copy(ufin.at[j, portion(s)], ufin.at[j, portion(s)], gs.at[j, d - 1], gr.at[j, d - 1], across(d))

    ri = lax.broadcasted_iota(jnp.int32, (B, B), 0)
    ci = lax.broadcasted_iota(jnp.int32, (B, B), 1)
    rows8 = lax.broadcasted_iota(jnp.int32, (8, B), 0)
    offs, tail = spots(wb)

    def update_out(j):
        for h in range(parts):
            rr = pl.ds(j * SW + h * tm, tm)
            for e in range(1, ns):
                for k in range(per):
                    q_copy(e, k, j, h).wait_recv()
                    prod_ref[rr, pl.ds(k * pw, pw)] += qrecv[e - 1, k, rr]
        extra = jnp.zeros((8, B), F32)
        held = None
        for i in range(wb):
            qh, ql = split(prod_ref[pl.ds(j * SW + i * B, B)])
            rest = pl.ds(j * SW + i * B, SW - i * B)
            line = dot3(qh, ql, ph[0, rest], plo[0, rest], NT)
            for k in range(i + 1, wb):
                upack[j, pl.ds(offs[i, k], B)] = line[:, (k - i) * B:(k - i + 1) * B]
            if i % 2 == 0:
                held = line[:, :B]
            else:
                low = line[:, :B]
                upack[j, pl.ds(i // 2 * B, B)] = jnp.where(ri <= ci, held, low)
                mid = jnp.sum(jnp.where(ri == ci, low, 0.0), axis=0, keepdims=True)
                extra = jnp.where(rows8 == i // 2, mid, extra)
        upack[j, pl.ds(tail, 8)] = extra
        upack[j, pl.ds(tail + 8, 8 * (nrow - 1))] = jnp.zeros((8 * (nrow - 1), B), F32)
        for d in range(1, ns):
            u_copy(j, d).start()

    def negate(j):
        for i in range(wb):
            here = pl.ds(j * SW + i * B, B)
            for c in range(blocks):
                cols = pl.ds(c * B, B)
                prod_ref[here, cols] = prod_ref[here, cols] * -(inside(j, i) * present(j, row, c))

    def second(j):
        negate(j)
        for d in range(1, ns):
            u_copy(j, d).wait_recv()
        total = upack[j, portion(s)]
        for d in range(1, ns):
            total += urecv[j, d - 1]
        usum[j] = total
        for d in range(1, nf):
            v_copy(j, d).start()

    def third(j):
        for d in range(1, nf):
            v_copy(j, d).wait_recv()
        total = usum[j, pl.ds(pl.multiple_of(f * part, 8), part)]
        for d in range(1, nf):
            total += urecv2[j, d - 1]
        ufin[j, pl.ds(pl.multiple_of((s * nf + f) * part, 8), part)] = total
        for d in range(1, nf):
            h_copy(j, d).start()

    def fourth(j):
        for d in range(1, nf):
            h_copy(j, d).wait_recv()
        for d in range(1, ns):
            g_copy(j, d).start()

    def finish(j):
        for d in range(1, ns):
            g_copy(j, d).wait_recv()
        sum_ref[j] = ufin[j]
        for i in range(wb):
            sum_ref[j, pl.ds(tail + 8 + i, 1)] = jnp.broadcast_to(inside(j, i), (1, B))

    stages = [update_out, second, third, fourth]
    for step in range(slots - 1 + len(stages)):
        for j in reversed(range(slots)):
            if 0 <= step - j < len(stages):
                stages[step - j](j)
    for j in range(slots):
        finish(j)

    for j in range(slots):
        for d in range(1, ns):
            u_copy(j, d).wait_send()
            g_copy(j, d).wait_send()
        for d in range(1, nf):
            v_copy(j, d).wait_send()
            h_copy(j, d).wait_send()
        for h in range(parts):
            for e in range(1, ns):
                for k in range(per):
                    q_copy(e, k, j, h).wait_send()
            for d in range(1, nf):
                panel_copy(d, j, h).wait_send()

    if crossed is None:
        for d in range(1, nf):
            for e in range(1, ns):
                for k in range(per):
                    opp_copy(anc_ref, d, e, k).wait_send()

    def drain(q, carry):
        p = sec * ncol + q
        to_right = jnp.logical_and(q <= col, col < ncol - 1)
        to_left = jnp.logical_and(q >= col, col > 0)
        if crossed is None:
            sent = q >= 0
        else:
            sent = jnp.logical_or(early(sec, q), late(p))
        pl.when(jnp.logical_and(sent, to_right))(lambda: piece_copy(anc_ref, p, 1).wait_send())
        pl.when(jnp.logical_and(sent, to_left))(lambda: piece_copy(anc_ref, p, 0).wait_send())
        pl.when(sent)(lambda: piece_copy(anc_ref, p, 2).wait_send())
        if crossed is not None:
            first_half = early(sec, q)
            pl.when(jnp.logical_and(first_half, to_right))(lambda: o_copy(q, 1).wait_send())
            pl.when(jnp.logical_and(first_half, to_left))(lambda: o_copy(q, 0).wait_send())
            pl.when(first_half)(lambda: o_copy(q, 2).wait_send())
        return carry

    lax.fori_loop(0, ncol, drain, 0)
    if crossed is not None:
        @pl.when(is_opp)
        def _():
            cross_copies(0).wait_send()
            cross_copies(1).wait_send()


def write_out(parts, prod_ref, sum_ref, diag_ref, off_ref, upd_ref):
    h = pl.program_id(1)
    wb = SW // B
    each = wb // parts
    offs, tail = spots(wb)
    ri = lax.broadcasted_iota(jnp.int32, (B, B), 0)
    ci = lax.broadcasted_iota(jnp.int32, (B, B), 1)
    off_ref[...] = prod_ref[...]

    def inside(i):
        return sum_ref[0, pl.ds(tail + 8 + i, 1)]

    def block_of(i, k):
        if i < k:
            return sum_ref[0, pl.ds(offs[i, k], B)]
        if i > k:
            return sum_ref[0, pl.ds(offs[k, i], B)].T
        both = sum_ref[0, pl.ds(i // 2 * B, B)]
        if i % 2 == 0:
            return jnp.where(ri <= ci, both, both.T)
        return jnp.where(ri == ci, sum_ref[0, pl.ds(tail + i // 2, 1)], jnp.where(ri > ci, both, both.T))

    for part in range(parts):
        @pl.when(h == part)
        def _():
            for i in range(each):
                for k in range(wb):
                    here = (pl.ds(i * B, B), pl.ds(k * B, B))
                    upd_ref[here] = (diag_ref[here] + block_of(part * each + i, k)) * inside(max(part * each + i, k))


def local(sizes, anc_inverse, panel, diag_inverse, widths, pattern):
    nsec, nrow, ncol, nf, ns, nb, square = sizes
    rows, width = panel.shape
    pw = anc_inverse.shape[1]
    per = width // pw
    slots = rows // SW
    pieces = nsec * ncol
    packed = packed_rows(nrow)
    part = packed // nrow
    parts = SW // TM
    short = square and nsec == nb == per == 2 and ncol == per * nb
    vm = pltpu.VMEM
    dma = pltpu.SemaphoreType.DMA
    whole = pl.BlockSpec(memory_space=pltpu.VMEM)
    far = pl.BlockSpec(memory_space=pltpu.HBM)
    product, summed = pl.pallas_call(
        functools.partial(kernel, sizes),
        out_shape=(jax.ShapeDtypeStruct((rows, width), F32), jax.ShapeDtypeStruct((slots, packed, B), F32)),
        in_specs=[far, far, far, far],
        out_specs=(whole, whole),
        scratch_shapes=[
            vm((pieces, width, pw), F32),
            vm((pieces, width, pw), BF),
            vm((pieces, width, pw), BF),
            vm((nf, rows, width), BF),
            vm((nf, rows, width), BF),
            vm((nf - 1, slots, SW, width), F32),
            None if short else vm((nf - 1, ns - 1, per, width, pw), F32),
            vm((nf - 1, ns - 1, per, width, pw), BF),
            vm((nf - 1, ns - 1, per, width, pw), BF),
            vm((ns - 1, per, rows, pw), F32),
            vm((ns - 1, per, rows, pw), F32),
            vm((slots, packed, B), F32),
            vm((slots, ns - 1, nf * part, B), F32),
            vm((slots, nf * part, B), F32),
            vm((slots, nf - 1, part, B), F32),
            vm((slots, packed, B), F32),
            dma((pieces, 3, CHUNKS)), dma((pieces, CHUNKS)),
            dma((nf - 1, slots, parts)), dma((nf - 1, slots, parts)),
            None if short else dma((nf - 1, ns - 1, per)), None if short else dma((nf - 1, ns - 1, per)),
            dma((ns - 1, per, slots, parts)), dma((ns - 1, per, slots, parts)),
            dma((slots, ns - 1)), dma((slots, ns - 1)),
            dma((slots, nf - 1)), dma((slots, nf - 1)),
            dma((slots, nf - 1)), dma((slots, nf - 1)),
            dma((slots, ns - 1)), dma((slots, ns - 1)),
            vm((width, pw), F32), vm((rows, width), F32),
            pltpu.SMEM(widths.shape, widths.dtype), pltpu.SMEM(pattern.shape, pattern.dtype), dma((4,)),
            (
                vm((ncol, width // 2, pw), F32), dma((2, OCHUNKS)), dma((OCHUNKS,)),
                dma((ncol, 3, OCHUNKS)), dma((ncol, OCHUNKS)),
            ) if short else None,
        ],
        compiler_params=pltpu.CompilerParams(
            collective_id=0, has_side_effects=True, vmem_limit_bytes=(49 if short else 60) * 1024 * 1024
        ),
    )(*(pltpu.with_memory_space_constraint(x, pltpu.HBM) for x in (anc_inverse, panel, widths, pattern)))
    strip = pl.BlockSpec((TM, width), lambda j, h: (j * parts + h, 0))
    square_strip = pl.BlockSpec((TM, SW), lambda j, h: (j * parts + h, 0))
    return pl.pallas_call(
        functools.partial(write_out, parts),
        grid=(slots, parts),
        out_shape=(jax.ShapeDtypeStruct((rows, width), F32), jax.ShapeDtypeStruct((rows, SW), F32)),
        in_specs=[strip, pl.BlockSpec((1, packed, B), lambda j, h: (j, 0, 0)), square_strip],
        out_specs=(strip, square_strip),
        compiler_params=pltpu.CompilerParams(vmem_limit_bytes=16 * 1024 * 1024),
    )(product, summed, diag_inverse)


def solution(mesh):
    shape = dict(mesh.shape)
    na, nb = factor(shape["row"])
    sizes = (shape["sec"], shape["row"], shape["col"], na, nb, nb, na == nb)
    in_specs = (
        P("row", ("sec", "col")),
        P(("sec", "col"), "row"),
        P(("sec", "col"), None),
        P(),
        P(),
    )
    out_specs = (P(("sec", "col"), "row"), P(("sec", "col"), None))
    return jax.shard_map(
        functools.partial(local, sizes), mesh=mesh, in_specs=in_specs, out_specs=out_specs, check_vma=False
    )
```
